128 devices in a mesh: section: 4 (over z_hi, core), dp: 32 (over z_lo, y, x).
Axes of the slice: x: 4, y: 4, z: 4 (z_hi: 2, z_lo: 2; z = z_hi * 2 + z_lo), core: 2. Of those that a mesh axis runs over, the one named last changes fastest.
Arguments:
- value_weight: bfloat16 [4, 8192, 1024], P('section', 'dp'), may hold values from -0.0625 to 0.0625
- norm_gain: bfloat16 [4, 8192], P('section'), may hold values from 0.25 to 1.75
- mask_logits: bfloat16 [4, 6, 2048, 1024], P('section', None, 'dp'), may hold values from -5 to 5
- gumbel_noise: bfloat16 [4, 6, 2048, 1024], P('section', None, 'dp'), may hold values from -2.23 to 9.22, as said below
- stream_in: bfloat16 [2, 2048, 8192], P(None, 'dp'), may hold values from -6 to 6
- stream_grad: bfloat16 [2, 2048, 8192], P(None, 'dp'), may hold values from -6 to 6
Outputs:
- logit_grad: bfloat16 [4, 6, 2048, 1024], P('section', None, 'dp')
The draws below stay inside these ranges and needn't reach their ends.
Inputs may be any that keep to these rules, and one draw needn't show every extreme that they name: `gumbel_noise`: gumbel noise, minus the log of minus the log of a uniform number.
All inputs are finite; a program needn't handle non-finite values.
Results may differ from the reference program's by a relative error of at most 0.029.
Values may be sent and summed in bfloat16 or wider, within the bound.
No kernel may reach another device: no remote copies, remote signals or barrier semaphores. Data moves between devices by JAX's collectives and lax.ppermute only.
A program may use at most 128 MiB of HBM per device.

```python
import jax
import jax.numpy as jnp
from jax import lax

D = 8192
KV = 1024
VHEADS = 8
MICRO = 2
TOK_DEV = 64
SECTIONS = 4
WORDPIECE_COUNT = 2048


def draw_gumbel_noise(key, part):
    uniform = jax.random.uniform(key, (SECTIONS, 6, D // 4, KV), jnp.float32, 0.0001, 1.0 - 0.0001)
    return (-jnp.log(-jnp.log(uniform))).astype(jnp.bfloat16)


def level_of(stream_key, dims, shards, least, high):
    loudness, own = 1.0, jax.random.fold_in(stream_key, 6)
    for position, blocks in shards:
        heights = jnp.exp(jax.random.uniform(jax.random.fold_in(own, position), (blocks,), jnp.float32, least / len(shards), high / len(shards)))
        loudness = loudness * jnp.repeat(heights, dims[position] // blocks).reshape([-1 if axis == position else 1 for axis in range(len(dims))])
    return loudness


def bell_draw(own_key, dims, scale, reach, shards=(), dtype=jnp.bfloat16):
    entries = jax.random.normal(own_key, dims, jnp.float32) * scale
    if len(shards) > 0:
        entries = level_of(own_key, dims, shards, -0.22, 0.18) * entries
    return jnp.clip(entries, min=-reach, max=reach).astype(dtype)


def setup_inputs(seed: int = 0) -> dict:
    splits = jax.random.split(jax.random.key(seed), 7)
    return {
        "value_weight": bell_draw(splits[0], (SECTIONS, D, KV), D ** -0.5, 0.0625, ((0, 4), (1, 32))),
        "norm_gain": jnp.clip(1.0 + 0.15 * jax.random.normal(splits[1], (SECTIONS, D), jnp.float32), 0.25, 1.75).astype(jnp.bfloat16),
        "mask_logits": bell_draw(splits[2], (SECTIONS, 6, D // 4, KV), 1.5, 5.0, ((0, 4), (2, 32))),
        "gumbel_noise": draw_gumbel_noise(jax.random.fold_in(splits[6], 71), 0),
        "stream_in": bell_draw(splits[4], (MICRO, WORDPIECE_COUNT, D), 1.0, 6.0, ((1, 32),)),
        "stream_grad": bell_draw(splits[5], (MICRO, WORDPIECE_COUNT, D), 1.0, 6.0, ((1, 32),)),
    }


sharpness_divisor = 0.6666667
epsilon = 1e-05

def soft_mask(keeping_propensity, perturbed_draw):
    ranking_measure = (keeping_propensity.astype(jnp.float32) + perturbed_draw.astype(jnp.float32)) / sharpness_divisor
    expo = jnp.exp(ranking_measure)
    probs = expo / lax.optimization_barrier(jnp.sum(expo, axis=0))
    first = probs[0] + probs[1] + probs[2]
    second = probs[0] + probs[3] + probs[4]
    third = probs[1] + probs[3] + probs[5]
    fourth = probs[2] + probs[4] + probs[5]
    mask = jnp.stack([first, second, third, fourth], axis=1)
    return (probs, mask.reshape(-1, mask.shape[-1]))

def mask_logit_backward(probs, weight, grads):
    dmask = (grads * weight.astype(jnp.float32)).reshape(-1, 4, grads.shape[-1])
    row_a, row_b, row_c, row_d = (dmask[:, 0], dmask[:, 1], dmask[:, 2], dmask[:, 3])
    dprob = jnp.stack([row_a + row_b, row_a + row_c, row_a + row_d, row_b + row_c, row_b + row_d, row_c + row_d])
    ranking_derivative = probs * (dprob - lax.optimization_barrier(jnp.sum(probs * dprob, axis=0)))
    return (ranking_derivative / sharpness_divisor).astype(jnp.bfloat16)

def norm_forward(stream, gain):
    values = stream.astype(jnp.float32)
    scale = lax.rsqrt(lax.optimization_barrier(jnp.mean(values * values, axis=-1, keepdims=True)) + epsilon)
    normed = (values * scale * gain).astype(jnp.bfloat16)
    return (values, scale, normed)

def expand(value, width):
    count = value.shape[0]
    head = value.shape[1] // VHEADS
    repeat = width // value.shape[1]
    grown = jnp.broadcast_to(value.reshape(count, VHEADS, 1, head), (count, VHEADS, repeat, head))
    return grown.reshape(count, width)

def collapse(grad, kv_width):
    count, width = grad.shape
    head = kv_width // VHEADS
    repeat = width // kv_width
    return lax.optimization_barrier(jnp.sum(grad.reshape(count, VHEADS, repeat, head), axis=2)).reshape(count, kv_width)

def norm_backward(values, scale, gain, dnormed):
    scaled = dnormed * gain
    return scale * scaled - values * (scale * scale * scale) * lax.optimization_barrier(jnp.mean(scaled * values, axis=-1, keepdims=True))

def reference(value_weight, norm_gain, mask_logits, gumbel_noise, stream_in, stream_grad):
    sections = value_weight.shape[0]
    micro, wordpiece_total, width = stream_in.shape
    kv_width = value_weight.shape[2]
    devices = wordpiece_total // TOK_DEV
    probs_list = []
    weights = []
    for layer in range(sections):
        probs, mask = soft_mask(mask_logits[layer], gumbel_noise[layer])
        probs_list.append(probs)
        weights.append((value_weight[layer].astype(jnp.float32) * mask).astype(jnp.bfloat16))
    saved_x = [[None] * micro for layer in range(sections)]
    saved_u = [[None] * micro for layer in range(sections)]
    saved_g = [[None] * micro for layer in range(sections)]
    for batch in range(micro):
        stream = stream_in[batch]
        for layer in range(sections):
            gain = norm_gain[layer].astype(jnp.float32)
            values, scale, normed = norm_forward(stream, gain)
            saved_x[layer][batch] = stream
            saved_u[layer][batch] = normed
            value = jnp.dot(normed, weights[layer], preferred_element_type=jnp.float32)
            stream = (values + expand(value, width)).astype(jnp.bfloat16)
    for batch in range(micro):
        grad = stream_grad[batch]
        for layer in range(sections - 1, -1, -1):
            gain = norm_gain[layer].astype(jnp.float32)
            upper = grad.astype(jnp.float32)
            vgrad = collapse(upper, kv_width).astype(jnp.bfloat16)
            saved_g[layer][batch] = vgrad
            dnormed = lax.dot_general(vgrad, weights[layer], (((1,), (1,)), ((), ())), preferred_element_type=jnp.float32)
            values, scale, normed = norm_forward(saved_x[layer][batch], gain)
            grad = (upper + norm_backward(values, scale, gain, dnormed)).astype(jnp.bfloat16)
    results = []
    for layer in range(sections):
        inputs = jnp.stack(saved_u[layer]).reshape(micro, devices, TOK_DEV, width)
        inputs = jnp.transpose(inputs, (1, 0, 2, 3)).reshape(devices, micro * TOK_DEV, width)
        payload_derivatives = jnp.stack(saved_g[layer]).reshape(micro, devices, TOK_DEV, kv_width)
        payload_derivatives = jnp.transpose(payload_derivatives, (1, 0, 2, 3)).reshape(devices, micro * TOK_DEV, kv_width)

        def absorb(total, pair):
            term = lax.dot_general(pair[0], pair[1], (((0,), (0,)), ((), ())), preferred_element_type=jnp.float32)
            rounded = lax.optimization_barrier(term.astype(jnp.bfloat16))
            return (total + rounded.astype(jnp.float32), None)
        wgrad, discarded_value = lax.scan(absorb, jnp.zeros((width, kv_width), jnp.float32), (inputs, payload_derivatives))
        results.append(mask_logit_backward(probs_list[layer], value_weight[layer], wgrad))
    return jnp.stack(results)
```

```python
import jax
import jax.numpy as jnp
from jax import lax
from jax.sharding import Mesh
from jax.sharding import PartitionSpec as P

VHEADS = 8
sharpness_divisor = 0.6666667
epsilon = 1e-05
BF = jnp.bfloat16
F32 = jnp.float32
CHUNKS = 2
NEAR = [(z, k) for z in range(2) for k in range(4)]


def soft_mask(logits, noise):
    score = (logits.astype(F32) + noise.astype(F32)) / sharpness_divisor
    expo = jnp.exp(score)
    probs = expo / jnp.sum(expo, axis=0)
    first = probs[0] + probs[1] + probs[2]
    second = probs[0] + probs[3] + probs[4]
    third = probs[1] + probs[3] + probs[5]
    fourth = probs[2] + probs[4] + probs[5]
    mask = jnp.stack([first, second, third, fourth], axis=1)
    return probs, mask.reshape(-1, mask.shape[-1])


def mask_logit_backward(probs, weight, grads):
    dmask = (grads * weight.astype(F32)).reshape(-1, 4, grads.shape[-1])
    a, b, c, d = (dmask[:, r] for r in range(4))
    dprob = jnp.stack([a + b, a + c, a + d, b + c, b + d, c + d])
    out = probs * (dprob - jnp.sum(probs * dprob, axis=0))
    return (out / sharpness_divisor).astype(BF)


def swap(v, axis):
    return lax.ppermute(v, axis, [(0, 1), (1, 0)])


def to_near(v, z, k):
    pairs = [(a * 4 + b, (a ^ z) * 4 + (b + k) % 4) for a in range(2) for b in range(4)]
    return v if z == 0 and k == 0 else lax.ppermute(v, ("zl", "y"), pairs)


def along_x(v, k):
    return v if k == 0 else lax.ppermute(v, "x", [(i, (i + k) % 4) for i in range(4)])


def rows_of(v, block, size):
    return lax.dynamic_slice_in_dim(v, block * size, size, 0)


def cols_of(v, block, size):
    return lax.dynamic_slice_in_dim(v, block * size, size, v.ndim - 1)


def put(buffer, piece, *at):
    starts = list(at) + [0] * (buffer.ndim - len(at))
    return lax.dynamic_update_slice(buffer, piece, starts)


def per_device(value_weight, norm_gain, mask_logits, gumbel_noise, stream_in, stream_grad):
    zh, co, zl, y, x = (lax.axis_index(n) for n in ("zh", "co", "zl", "y", "x"))
    micro, rows, width = stream_in.shape
    kv = value_weight.shape[2]
    head = kv // VHEADS
    repeat = width // kv
    part = value_weight.shape[1]
    span = width // VHEADS
    kc = kv // CHUNKS
    own = zl * 16 + y * 4 + x
    core0 = co == 0

    mine = lax.dynamic_index_in_dim(stream_in, co, 0, keepdims=False)
    got = []
    for z, k in NEAR:
        to = (zl ^ z) * 4 + (y + k) % 4
        got.append(to_near(cols_of(mine, to, span), z, k))
    got = jnp.stack(got)
    xh = jnp.stack([got, swap(got, "co")])

    weight = value_weight[0].astype(F32)
    gain = rows_of(norm_gain[0].astype(F32), own, part)[:, None]
    probs, mask = soft_mask(mask_logits[0], gumbel_noise[0])
    scaled = (weight * mask * gain).astype(BF)
    full = []
    for j in range(CHUNKS):
        piece = scaled[:, j * kc : (j + 1) * kc]
        whole = jnp.zeros((span, kc), BF)
        for k in range(4):
            whole = put(whole, along_x(piece, k), (x - k) % 4 * part, 0)
        full.append(whole)

    flat = xh.reshape(-1, span)
    first = []
    for j in range(CHUNKS):
        u = jnp.dot(flat, full[j], preferred_element_type=F32).astype(BF)
        u = u.reshape(2, 8, rows, kc)
        total = None
        for i, (z, k) in enumerate(NEAR):
            back = (-k) % 4
            term = to_near(u[:, i], z, back).astype(F32)
            total = term if total is None else total + term
        first.append(total)
    first = jnp.concatenate(first, -1)

    quarter = head // 4
    short = []
    for j in range(CHUNKS):
        w = full[j].reshape(repeat, head, kc)
        w = lax.dynamic_slice_in_dim(w, x * quarter, quarter, 1)
        short.append(jnp.sum(w.astype(F32), axis=0).astype(BF))
    short = jnp.concatenate(short, -1)
    held = jnp.zeros((VHEADS, quarter, kv), BF)
    for z, k in NEAR:
        held = put(held, to_near(short, z, k)[None], (zl ^ z) * 4 + (y - k) % 4)
    square = jnp.zeros((VHEADS, 4, quarter, kv), BF)
    for k in range(4):
        square = put(square, along_x(held, k)[:, None], 0, (x - k) % 4)
    square = square.reshape(kv, kv)
    other = swap(square, "co")
    n_a = jnp.where(core0, square, other)
    n_b = jnp.where(core0, other, square)
    u_other = swap(first[1], "co")
    u_a = jnp.where(core0, first[0], u_other)
    u_b = jnp.where(core0, u_other, first[0])

    tokens = mine.astype(F32).reshape(rows, VHEADS, repeat, head)
    y0 = jnp.sum(tokens, axis=2)
    spread = jnp.sum(jnp.square(tokens - y0[:, :, None] / repeat), axis=(1, 2, 3))[:, None]
    y0 = y0.reshape(rows, kv)
    g4 = lax.dynamic_index_in_dim(stream_grad, co, 0, keepdims=False).astype(F32)
    g4 = jnp.sum(g4.reshape(rows, VHEADS, repeat, head), axis=2).reshape(rows, kv)

    def layer(c, u, n):
        sums = y0 + repeat * c
        mean = (spread + jnp.sum(sums * sums, -1, keepdims=True) / repeat) / width
        sigma = lax.rsqrt(mean + epsilon)
        value = sigma * (u + jnp.dot(c.astype(BF), n, preferred_element_type=F32))
        return sums, sigma, value

    def forward(c):
        sums_a, sigma_a, v_a = layer(c, u_a, n_a)
        mid = c + v_a
        sums_b, sigma_b, v_b = layer(mid, u_b, n_b)
        return (sums_a, sigma_a, v_a, n_a), (sums_b, sigma_b, v_b, n_b), mid, mid + v_b

    def back(g, saved):
        sums, sigma, value, n = saved
        vg = g.astype(BF)
        vf = vg.astype(F32)
        du = lax.dot_general(vg, n, (((1,), (1,)), ((), ())), preferred_element_type=F32)
        dot = jnp.sum(vf * value, -1, keepdims=True)
        lower = g + sigma * du - sigma * sigma * (dot / width) * sums
        return (sigma * vf).astype(BF), lower

    def backward(g, a, b):
        s_b, g = back(g, b)
        s_a, g = back(g, a)
        return s_a, s_b, g

    low = zh == 0
    c_out = forward(jnp.zeros((rows, kv), F32))[3]
    c_in = jnp.where(low, 0.0, swap(c_out.astype(BF), "zh").astype(F32))
    a, b, mid, _ = forward(c_in)
    g_out = backward(g4, a, b)[2]
    g_in = jnp.where(low, swap(g_out.astype(BF), "zh").astype(F32), g4)
    s_a, s_b, _ = backward(g_in, a, b)

    pair_a = jnp.stack([s_a, c_in.astype(BF)])
    pair_b = jnp.stack([s_b, mid.astype(BF)])
    keep = jnp.where(core0, pair_a, pair_b)
    take = swap(jnp.where(core0, pair_b, pair_a), "co")
    sv = jnp.stack([keep[0], take[0]])
    cs = jnp.stack([keep[1], take[1]])
    add = []
    for z, k in NEAR:
        to = (zl ^ z) * 4 + (y + k) % 4
        add.append(to_near(cols_of(cs, to, head), z, k))
    add = jnp.stack(add, 1).reshape(-1, head)
    xs = (flat.astype(F32) + jnp.tile(add, (1, repeat)).astype(F32)).astype(BF)

    wgrad = []
    for j in range(CHUNKS):
        piece = sv[:, :, j * kc : (j + 1) * kc]
        right = jnp.stack([to_near(piece, z, k) for z, k in NEAR], 1).reshape(-1, kc)
        term = lax.dot_general(xs, right, (((0,), (0,)), ((), ())), preferred_element_type=F32)
        term = term.astype(BF)
        total = None
        for k in range(4):
            got = along_x(rows_of(term, (x + k) % 4, part), k).astype(F32)
            total = got if total is None else total + got
        wgrad.append(total)
    wgrad = jnp.concatenate(wgrad, -1) * gain
    return mask_logit_backward(probs, value_weight[0], wgrad)[None]


def solution(mesh):
    fine = Mesh(mesh.devices.reshape(2, 2, 2, 4, 4), ("zh", "co", "zl", "y", "x"))
    layer, dp = ("zh", "co"), ("zl", "y", "x")
    return jax.shard_map(
        per_device,
        mesh=fine,
        in_specs=(
            P(layer, dp, None),
            P(layer, None),
            P(layer, None, dp, None),
            P(layer, None, dp, None),
            P(None, dp, None),
            P(None, dp, None),
        ),
        out_specs=P(layer, None, dp, None),
        check_vma=False,
    )
```

```python
import functools

import jax
import jax.numpy as jnp
from jax import lax
from jax.experimental import pallas as pl
from jax.experimental.pallas import tpu as pltpu
from jax.sharding import Mesh
from jax.sharding import PartitionSpec as P


VHEADS = 8
sharpness_divisor = 0.6666667
epsilon = 1e-05
BF = jnp.bfloat16
F32 = jnp.float32
CHUNKS = 2
INTERPRET = False
KEEPS = ((0, 1), (0, 2), (0, 3), (1, 2), (1, 3), (2, 3))
LAYER = ("zh", "co")


def shape(dims, dtype):
    return jax.ShapeDtypeStruct(dims, dtype)


def call(kernel, out, **rest):
    params = pltpu.CompilerParams(vmem_limit_bytes=20 << 20)
    return pl.pallas_call(kernel, out_shape=out, interpret=INTERPRET, compiler_params=params, **rest)


def tiles(width, most=128):
    step = min(width, most)
    return [slice(i, i + step) for i in range(0, width, step)]


def by_tile(rows, width, most=128):
    cols = tiles(width, min(most, 128))
    return pltpu.VMEM((len(cols), rows, cols[0].stop), F32)


def mask_kernel(at, logits, noise, weight, gain, probs, scaled, q0, q1, q2, q3, rows):
    for i, s in enumerate(tiles(weight.shape[1])):
        expo = [
            jnp.exp((logits[k, :, s].astype(F32) + noise[k, :, s].astype(F32)) * (1.0 / sharpness_divisor))
            for k in range(6)
        ]
        inverse = 1.0 / (((expo[0] + expo[1]) + (expo[2] + expo[3])) + (expo[4] + expo[5]))
        p = [e * inverse for e in expo]
        for k in range(6):
            probs[k, :, s] = p[k]
        for r in range(4):
            kept = [p[k] for k in range(6) if r in KEEPS[k]]
            rows.at[i][pl.ds(r, kept[0].shape[0], stride=4), :] = kept[0] + kept[1] + kept[2]
        value = weight[:, s].astype(F32) * rows[i] * gain[...]
        scaled[:, s] = value.astype(BF)
        rows[i] = value
        quarter = q0.shape[0]
        for k, q in enumerate((q0, q1, q2, q3)):
            begin = pl.multiple_of(lax.rem(at[0] + k, 4) * quarter, quarter)
            one = rows.at[i][pl.ds(begin, quarter), :]
            two = rows.at[i][pl.ds(begin + 4 * quarter, quarter), :]
            q[:, s] = (one + two).astype(BF)


def masked_weights(at, logits, noise, weight, gain):
    n, kv = weight.shape
    return call(
        mask_kernel,
        (shape(logits.shape, F32), shape((n, kv), BF)) + (shape((n // 8, kv), BF),) * 4,
        in_specs=[pl.BlockSpec(memory_space=pltpu.SMEM)] + [pl.BlockSpec(memory_space=pltpu.VMEM)] * 4,
        scratch_shapes=[by_tile(n, kv)],
    )(at, logits, noise, weight, gain)


def final_kernel(probs, weight, gain, *refs):
    parts, out, rows = refs[:-2], refs[-2], refs[-1]
    kv = weight.shape[1]
    wide = parts[0].shape[1]
    for i, s in enumerate(tiles(kv, min(wide, 128))):
        j, at = divmod(s.start, wide)
        inner = slice(at, at + s.stop - s.start)
        mine = parts[j * 4 : j * 4 + 4]
        total = (mine[0][:, inner].astype(F32) + mine[1][:, inner].astype(F32)) + (
            mine[2][:, inner].astype(F32) + mine[3][:, inner].astype(F32)
        )
        rows[i] = total * gain[...] * weight[:, s].astype(F32) * (1.0 / sharpness_divisor)
        d = [rows.at[i][pl.ds(r, probs.shape[1], stride=4), :] for r in range(4)]
        p = [probs[k, :, s] for k in range(6)]
        dprob = [d[a] + d[b] for a, b in KEEPS]
        mean = p[0] * dprob[0]
        for k in range(1, 6):
            mean = mean + p[k] * dprob[k]
        for k in range(6):
            out[k, :, s] = (p[k] * (dprob[k] - mean)).astype(BF)


def logit_gradient(probs, weight, gain, parts):
    return call(
        final_kernel,
        shape(probs.shape, BF),
        scratch_shapes=[by_tile(*weight.shape, most=parts[0].shape[1])],
    )(probs, weight, gain, *parts)


def sums_kernel(repeat, head, core, tokens, grads, y0, spread, g4, mine):
    t = tokens[0]
    mine[0] = t
    pieces = [t[:, r * head : (r + 1) * head].astype(F32) for r in range(repeat)]
    total = functools.reduce(lambda a, b: a + b, pieces)
    mean = total * (1.0 / repeat)
    squares = functools.reduce(lambda a, b: a + b, [(p - mean) * (p - mean) for p in pieces])
    y0[...] = total

    @pl.when(pl.program_id(0) == 0)
    def _():
        spread[...] = squares

    @pl.when(pl.program_id(0) != 0)
    def _():
        spread[...] += squares

    g = grads[0]
    g4[...] = functools.reduce(
        lambda a, b: a + b, [g[:, r * head : (r + 1) * head].astype(F32) for r in range(repeat)]
    )


def token_sums(core, tokens, grads, head):
    rows, width = tokens.shape[1:]
    span = width // VHEADS
    block = pl.BlockSpec((1, rows, span), lambda h, core: (core[0], 0, h))
    narrow = pl.BlockSpec((rows, head), lambda h, core: (0, h))
    return call(
        functools.partial(sums_kernel, span // head, head),
        (
            shape((rows, VHEADS * head), F32),
            shape((rows, head), F32),
            shape((rows, VHEADS * head), F32),
            shape((VHEADS, rows, span), tokens.dtype),
        ),
        grid_spec=pltpu.PrefetchScalarGridSpec(
            num_scalar_prefetch=1,
            grid=(VHEADS,),
            in_specs=[block, block],
            out_specs=(
                narrow,
                pl.BlockSpec((rows, head), lambda h, core: (0, 0)),
                narrow,
                pl.BlockSpec((1, rows, span), lambda h, core: (h, 0, 0)),
            ),
        ),
    )(core, tokens, grads)


def values_kernel(at, core, own, other, w0, w1, w3, top, bottom, u):
    part = w0.shape[0]
    mine = core[0] == pl.program_id(0) // 2
    total = None
    opposite = jnp.concatenate([top[...], bottom[...]], 0)
    for k, w in enumerate((w0, w1, opposite, w3)):
        cols = pl.ds(pl.multiple_of(lax.rem(at[0] - k + 4, 4) * part, part), part)
        tokens = jnp.where(mine, own[:, cols], other[:, cols])
        term = jnp.dot(tokens, w[...], preferred_element_type=F32)
        total = term if total is None else total + term
    u[...] = total.astype(BF)


def turn_over_kernel(core, own, other, turned):
    turned[...] = jnp.where(core[0] == pl.program_id(0) // 2, own[...], other[...]).T


def partial_values(at, core, own, other, blocks):
    count, span = own.shape
    kv = blocks[0].shape[1]
    step = count // 2
    tokens = pl.BlockSpec((step, span), lambda i, at, core: (i % 2, 0))
    return call(
        values_kernel,
        shape((2 * count, kv), BF),
        grid_spec=pltpu.PrefetchScalarGridSpec(
            num_scalar_prefetch=2,
            grid=(4,),
            in_specs=[tokens, tokens]
            + [pl.BlockSpec(b.shape, lambda i, at, core: (0, 0)) for b in blocks],
            out_specs=pl.BlockSpec((step, kv), lambda i, at, core: (i, 0)),
        ),
    )(at, core, own, other, *blocks)


def turn_over(core, own, other):
    count, span = own.shape
    step = count // 2
    tokens = pl.BlockSpec((step, span), lambda i, core: (i % 2, 0))
    return call(
        turn_over_kernel,
        shape((span, 2 * count), BF),
        grid_spec=pltpu.PrefetchScalarGridSpec(
            num_scalar_prefetch=1,
            grid=(4,),
            in_specs=[tokens, tokens],
            out_specs=pl.BlockSpec((span, step), lambda i, core: (0, i)),
        ),
    )(core, own, other)


def short_kernel(q0, q1, q2, q3, out):
    total = (q0[...].astype(F32) + q1[...].astype(F32)) + (q2[...].astype(F32) + q3[...].astype(F32))
    out[...] = jnp.broadcast_to(total.astype(BF), out.shape)


def short_weights(quarters):
    return call(short_kernel, shape((VHEADS, *quarters[0].shape), BF))(*quarters)


def square_kernel(at, n0, n1, n2, n3, out):
    heads, quarter = n0.shape[:2]
    for k, n in enumerate((n0, n1, n2, n3)):
        source = lax.rem(at[0] - k + 4, 4)
        for h in range(heads):
            begin = pl.multiple_of(h * 4 * quarter + source * quarter, quarter)
            out[pl.ds(begin, quarter), :] = n[h]


def square_weights(at, blocks):
    kv = blocks[0].shape[2]
    return call(
        square_kernel,
        shape((kv, kv), BF),
        in_specs=[pl.BlockSpec(memory_space=pltpu.SMEM)] + [pl.BlockSpec(memory_space=pltpu.VMEM)] * 4,
    )(at, *blocks)


def scale_of(sums, spread, repeat, width):
    mean = jnp.sum(spread, -1, keepdims=True) + jnp.sum(sums * sums, -1, keepdims=True) * (1.0 / repeat)
    return lax.rsqrt(mean * (1.0 / width) + epsilon)


def by_layer(core, layer, own, other, acc, v, dims):
    @pl.when(core == layer)
    def _():
        acc[...] = lax.dot_general(v, own[...], (dims, ((), ())), preferred_element_type=F32)

    @pl.when(core != layer)
    def _():
        acc[...] = lax.dot_general(v, other[...], (dims, ((), ())), preferred_element_type=F32)

    return acc[...]


AHEAD = ((1,), (0,))
BEHIND = ((1,), (1,))


def first_kernel(repeat, width, at, own, other, parts, y0, spread, u, c_out, acc):
    count = parts.shape[0] // 2
    for layer in range(2):
        total = parts[layer * count].astype(F32)
        for i in range(1, count):
            total = total + parts[layer * count + i].astype(F32)
        u[layer] = total
    c = scale_of(y0[...], spread[...], repeat, width) * u[0]
    sums = y0[...] + repeat * c
    value = u[1] + by_layer(at[0], 1, own, other, acc, c.astype(BF), AHEAD)
    c_out[...] = (c + scale_of(sums, spread[...], repeat, width) * value).astype(BF)


def lower_of(width, at, layer, own, other, acc, g, sums, sigma, value):
    vg = g.astype(BF)
    du = by_layer(at[0], layer, own, other, acc, vg, BEHIND)
    dot = jnp.sum(vg.astype(F32) * value, -1, keepdims=True) * (1.0 / width)
    return g + sigma * du - sigma * sigma * dot * sums


def turn_kernel(repeat, width, at, own, other, u, y0, spread, c_in, g4, value, sums, sigma, mid, g_out, acc):
    c = c_in[...]
    base = c.astype(F32)
    for layer in range(2):
        sums[layer] = y0[...] + repeat * base
        s = scale_of(sums[layer], spread[...], repeat, width)
        sigma[layer] = jnp.broadcast_to(s, sigma.shape[1:])
        value[layer] = s * (u[layer] + by_layer(at[0], layer, own, other, acc, c, AHEAD))
        if layer == 0:
            base = base + value[0]
            c = base.astype(BF)
            mid[...] = c
    g = g4[...]
    for layer in (1, 0):
        g = lower_of(width, at, layer, own, other, acc, g, sums[layer], sigma[layer][:, :1], value[layer])
    g_out[...] = g.astype(BF)


def send_kernel(width, kc, at, own, other, g4, g_in, value, sums, sigma, c_in, mid, *outs):
    outs, acc = outs[:-1], outs[-1]
    head = c_in.shape[1] // VHEADS
    g = jnp.where(at[1] == 1, g4[...], g_in[...].astype(F32))
    for layer in (1, 0):
        s = sigma[layer][:, :1]
        sv = (g.astype(BF).astype(F32) * s).astype(BF)
        c = (c_in, mid)[layer]
        for i in range(VHEADS):
            for j, out in enumerate(outs):
                out[layer * VHEADS + i, :, :kc] = sv[:, j * kc : (j + 1) * kc]
            outs[0][layer * VHEADS + i, :, kc:] = c[:, i * head : (i + 1) * head]
        if layer == 1:
            g = lower_of(width, at, 1, own, other, acc, g, sums[1], s, value[1])


def chain_call(kernel, out, at, *args):
    rows, kv = args[2].shape[-2:]
    return call(
        kernel,
        out,
        in_specs=[pl.BlockSpec(memory_space=pltpu.SMEM)] + [pl.BlockSpec(memory_space=pltpu.VMEM)] * len(args),
        scratch_shapes=[pltpu.VMEM((rows, kv), F32)],
    )(at, *args)


def wgrad_kernel(kc, at, turned, right, *outs):
    count = turned.shape[1]
    r = right[...].reshape(count, right.shape[2])
    part = outs[0].shape[0]
    if r.shape[1] > kc:
        c = r[:, kc:].astype(F32).T
        add = jnp.concatenate([c] * (part // c.shape[0]), 0)
    for k in range(4):
        rows = pl.ds(pl.multiple_of(lax.rem(at[0] + k, 4) * part, part), part)
        x = turned[rows, :]
        if r.shape[1] > kc:
            x = (x.astype(F32) + add).astype(BF)
            outs[4][rows, :] = x
        outs[k][...] = jnp.dot(x, r[:, :kc], preferred_element_type=F32).astype(BF)


def wgrad(at, turned, right, kc):
    span, count = turned.shape
    out = [shape((span // 4, kc), BF)] * 4
    if right.shape[2] > kc:
        out.append(shape((span, count), BF))
    return call(
        functools.partial(wgrad_kernel, kc),
        out,
        in_specs=[pl.BlockSpec(memory_space=pltpu.SMEM)] + [pl.BlockSpec(memory_space=pltpu.VMEM)] * 2,
    )(at, turned, right)


def along_x(v, k):
    return v if k == 0 else lax.ppermute(v, "x", [(i, (i + k) % 4) for i in range(4)])


def group(v, axes=("zl", "y")):
    return lax.all_to_all(v, axes, 0, 0, tiled=True)


def per_device(value_weight, norm_gain, mask_logits, gumbel_noise, stream_in, stream_grad):
    zh, co, zl, y, x = (lax.axis_index(n) for n in ("zh", "co", "zl", "y", "x"))
    _, rows, width = stream_in.shape
    kv = value_weight.shape[2]
    head = kv // VHEADS
    repeat = width // kv
    part = value_weight.shape[1]
    span = width // VHEADS
    kc = kv // CHUNKS
    own = zl * 16 + y * 4 + x
    at, core = x.reshape(1), co.reshape(1)
    weight = value_weight[0]
    gain = lax.dynamic_slice_in_dim(norm_gain[0].astype(F32), own * part, part, 0)[:, None]

    probs, scaled, *quarters = masked_weights(at, mask_logits[0], gumbel_noise[0], weight, gain)
    y0, spread, g4, mine = token_sums(core, stream_in, stream_grad, head)
    quarters = [along_x(quarters[k], k) for k in range(4)]
    short = short_weights(quarters)

    mine, scaled = lax.optimization_barrier((mine, scaled))
    before, after = along_x(scaled, 1), along_x(scaled, 3)
    blocks = [scaled, before, after, along_x(before[: part // 2], 1), along_x(after[part // 2 :], 3)]
    got = group(mine)
    swapped = lax.ppermute(got, "co", [(0, 1), (1, 0)])
    got, swapped = got.reshape(-1, span), swapped.reshape(-1, span)
    held = group(short)

    u = partial_values(at, core, got, swapped, blocks)
    u, held = lax.optimization_barrier((u, held))
    parts = group(u.reshape(2 * VHEADS, rows, kv), ("co", "zl", "y"))
    square = [along_x(held, k) for k in range(4)]
    turned = turn_over(core, got, swapped)
    n = square_weights(at, square)
    n_other = lax.ppermute(n, "co", [(0, 1), (1, 0)])

    where = jnp.stack([co, zh])
    two = shape((2, rows, kv), F32)
    half = shape((rows, kv), BF)
    u, c = chain_call(functools.partial(first_kernel, repeat, width), (two, half), where, n, n_other, parts, y0, spread)
    c_in = lax.ppermute(c, "zh", [(0, 1)])
    value, sums, sigma, mid, g = chain_call(
        functools.partial(turn_kernel, repeat, width),
        (two, two, shape((2, rows, head), F32), half, half),
        where, n, n_other, u, y0, spread, c_in, g4,
    )
    g_in = lax.ppermute(g, "zh", [(1, 0)])
    sends = chain_call(
        functools.partial(send_kernel, width, kc),
        tuple(shape((2 * VHEADS, rows, kc + (head if j == 0 else 0)), BF) for j in range(CHUNKS)),
        where, n, n_other, g4, g_in, value, sums, sigma, c_in, mid,
    )

    pieces = []
    for j in range(CHUNKS):
        right = group(sends[j], ("co", "zl", "y"))
        right, *pieces = lax.optimization_barrier((right, *pieces))
        term = wgrad(at, turned, right, kc)
        if j == 0:
            turned = term[4]
        pieces += [along_x(term[k], k) for k in range(4)]
    return logit_gradient(probs, weight, gain, pieces)[None]


def solution(mesh):
    fine = Mesh(mesh.devices.reshape(2, 2, 2, 4, 4), ("zh", "co", "zl", "y", "x"))
    dp = ("zl", "y", "x")

    return jax.shard_map(
        per_device,
        mesh=fine,
        in_specs=(
            P(LAYER, dp, None),
            P(LAYER, None),
            P(LAYER, None, dp, None),
            P(LAYER, None, dp, None),
            P(None, dp, None),
            P(None, dp, None),
        ),
        out_specs=P(LAYER, None, dp, None),
        check_vma=False,
    )
```

```python
import functools

import jax
import jax.numpy as jnp
from jax import lax
from jax.experimental import pallas as pl
from jax.experimental.pallas import tpu as pltpu
from jax.sharding import Mesh
from jax.sharding import PartitionSpec as P


VHEADS = 8
sharpness_divisor = 0.6666667
epsilon = 1e-05
BF = jnp.bfloat16
F32 = jnp.float32
INTERPRET = False
KEEPS = ((0, 1), (0, 2), (0, 3), (1, 2), (1, 3), (2, 3))
LAYER = ("zh", "co")


def shape(dims, dtype):
    return jax.ShapeDtypeStruct(dims, dtype)


def call(kernel, out, **rest):
    params = pltpu.CompilerParams(vmem_limit_bytes=20 << 20)
    return pl.pallas_call(kernel, out_shape=out, interpret=INTERPRET, compiler_params=params, **rest)


def tiles(width, most=128):
    step = min(width, most)
    return [slice(i, i + step) for i in range(0, width, step)]


def by_tile(rows, width, most=128):
    cols = tiles(width, min(most, 128))
    return pltpu.VMEM((len(cols), rows, cols[0].stop), F32)


def pattern_probs(logits, noise, s):
    expo = [
        jnp.exp((logits[k, :, s].astype(F32) + noise[k, :, s].astype(F32)) * (1.0 / sharpness_divisor))
        for k in range(6)
    ]
    inverse = 1.0 / (((expo[0] + expo[1]) + (expo[2] + expo[3])) + (expo[4] + expo[5]))
    return [e * inverse for e in expo]


def mask_kernel(at, logits, noise, weight, gain, scaled, q0, q1, q2, q3, rows):
    for i, s in enumerate(tiles(weight.shape[1])):
        p = pattern_probs(logits, noise, s)
        for r in range(4):
            kept = [p[k] for k in range(6) if r in KEEPS[k]]
            rows.at[i][pl.ds(r, kept[0].shape[0], stride=4), :] = kept[0] + kept[1] + kept[2]
        value = weight[:, s].astype(F32) * rows[i] * gain[...]
        scaled[:, s] = value.astype(BF)
        rows[i] = value
        quarter = q0.shape[0]
        for k, q in enumerate((q0, q1, q2, q3)):
            begin = pl.multiple_of(lax.rem(at[0] + k, 4) * quarter, quarter)
            one = rows.at[i][pl.ds(begin, quarter), :]
            two = rows.at[i][pl.ds(begin + 4 * quarter, quarter), :]
            q[:, s] = (one + two).astype(BF)


def masked_weights(at, logits, noise, weight, gain):
    n, kv = weight.shape
    return call(
        mask_kernel,
        (shape((n, kv), BF),) + (shape((n // 8, kv), BF),) * 4,
        in_specs=[pl.BlockSpec(memory_space=pltpu.SMEM)] + [pl.BlockSpec(memory_space=pltpu.VMEM)] * 4,
        scratch_shapes=[by_tile(n, kv)],
    )(at, logits, noise, weight, gain)


def final_kernel(logits, noise, weight, gain, *refs):
    parts, out, rows = refs[:-2], refs[-2], refs[-1]
    tile = rows.shape[2]
    where = [(j, at) for j in range(len(parts) // 4) for at in range(0, parts[j * 4].shape[1], tile)]
    for i, (j, at) in enumerate(where):
        s, inner = slice(i * tile, (i + 1) * tile), slice(at, at + tile)
        mine = parts[j * 4 : j * 4 + 4]
        total = (mine[0][:, inner].astype(F32) + mine[1][:, inner].astype(F32)) + (
            mine[2][:, inner].astype(F32) + mine[3][:, inner].astype(F32)
        )
        rows[i] = total * gain[...] * weight[:, s].astype(F32) * (1.0 / sharpness_divisor)
        d = [rows.at[i][pl.ds(r, logits.shape[1], stride=4), :] for r in range(4)]
        p = pattern_probs(logits, noise, s)
        dprob = [d[a] + d[b] for a, b in KEEPS]
        mean = p[0] * dprob[0]
        for k in range(1, 6):
            mean = mean + p[k] * dprob[k]
        for k in range(6):
            out[k, :, s] = (p[k] * (dprob[k] - mean)).astype(BF)


def logit_gradient(logits, noise, weight, gain, parts):
    return call(
        final_kernel,
        shape(logits.shape, BF),
        scratch_shapes=[by_tile(*weight.shape, most=weight.shape[1] // 8)],
    )(logits, noise, weight, gain, *parts)


def run_copies(copies, sems):
    copies = [pltpu.make_async_copy(src, dst, sems.at[i]) for i, (src, dst) in enumerate(copies)]
    for copy in copies:
        copy.start()
    for copy in copies:
        copy.wait()


def wide(index, part):
    return pl.ds(pl.multiple_of(index * part, part), part)


def place(core, zl, g, h):
    return zl * 16 + jnp.where(core == 0, g * 4 + h, h * 4 + g)


def heads_kernel(at, tokens, near, far, sems):
    zl, g, h, core = (at[i] for i in range(4))
    rows, width = tokens.shape[1:]
    part = width // 32
    copies = []
    for k in range(4):
        for i in range(4):
            source = wide(place(core, zl, lax.rem(g + k, 4), i), part)
            for m in range(2):
                copies.append((
                    tokens.at[core if m == 0 else 1 - core, :, source],
                    near.at[k, pl.ds(m * rows, rows), pl.ds(i * part, part)],
                ))
            source = wide(place(1 - core, 1 - zl, lax.rem(h + k, 4), i), part)
            copies.append((tokens.at[core, :, source], far.at[k, :, pl.ds(i * part, part)]))
    run_copies(copies, sems)


def token_blocks(at, tokens):
    rows, width = tokens.shape[1:]
    block = pl.BlockSpec(memory_space=pl.ANY)
    return call(
        heads_kernel,
        (shape((4, 2 * rows, width // 8), BF), shape((4, rows, width // 8), BF)),
        in_specs=[pl.BlockSpec(memory_space=pltpu.SMEM), block],
        out_specs=(block, block),
        scratch_shapes=[pltpu.SemaphoreType.DMA((48,))],
    )(at, tokens)


def pair_kernel(at, mine, other, o0, o1, o2, o3, sems):
    g, h = at[1], at[2]
    rows = mine.shape[1]
    part = mine.shape[2] // 4
    copies = []
    for k, out in enumerate((o0, o1, o2, o3)):
        for i in range(4):
            source = mine.at[lax.rem(i - h + 4, 4), :, wide(lax.rem(g + k, 4), part)]
            copies.append((source, out.at[pl.ds(0, rows), pl.ds(i * part, part)]))
        copies.append((other.at[k], out.at[pl.ds(rows, rows), :]))
    run_copies(copies, sems)


def pair_blocks(at, mine, other):
    rows, span = mine.shape[1:]
    block = pl.BlockSpec(memory_space=pl.ANY)
    return call(
        pair_kernel,
        (shape((2 * rows, span), BF),) * 4,
        in_specs=[pl.BlockSpec(memory_space=pltpu.SMEM), block, block],
        out_specs=(block,) * 4,
        scratch_shapes=[pltpu.SemaphoreType.DMA((20,))],
    )(at, mine, other)


def sums_kernel(repeat, head, core, tokens, grads, y0, spread, g4):
    t = tokens[0]
    pieces = [t[:, r * head : (r + 1) * head].astype(F32) for r in range(repeat)]
    total = functools.reduce(lambda a, b: a + b, pieces)
    mean = total * (1.0 / repeat)
    squares = functools.reduce(lambda a, b: a + b, [(p - mean) * (p - mean) for p in pieces])
    y0[...] = total

    @pl.when(pl.program_id(0) == 0)
    def _():
        spread[...] = squares

    @pl.when(pl.program_id(0) != 0)
    def _():
        spread[...] += squares

    g = grads[0]
    g4[...] = functools.reduce(
        lambda a, b: a + b, [g[:, r * head : (r + 1) * head].astype(F32) for r in range(repeat)]
    )


def token_sums(core, tokens, grads, head):
    rows, width = tokens.shape[1:]
    span = width // VHEADS
    block = pl.BlockSpec((1, rows, span), lambda h, core: (core[0], 0, h))
    narrow = pl.BlockSpec((rows, head), lambda h, core: (0, h))
    return call(
        functools.partial(sums_kernel, span // head, head),
        (
            shape((rows, VHEADS * head), F32),
            shape((rows, head), F32),
            shape((rows, VHEADS * head), F32),
        ),
        grid_spec=pltpu.PrefetchScalarGridSpec(
            num_scalar_prefetch=1,
            grid=(VHEADS,),
            in_specs=[block, block],
            out_specs=(
                narrow,
                pl.BlockSpec((rows, head), lambda h, core: (0, 0)),
                narrow,
            ),
        ),
    )(core, tokens, grads)


def small(count):
    vmem = pl.BlockSpec(memory_space=pltpu.VMEM)
    return dict(in_specs=[pl.BlockSpec(memory_space=pltpu.SMEM)] + [vmem] * count)


def values_kernel(at, *refs):
    tokens, w, outs = refs[:8], refs[8:12], refs[12:]
    part = w[0].shape[0]
    rows = tokens[0].shape[0]
    for k in range(4):
        total = None
        for j in range(4):
            cols = wide(lax.rem(at[2] - j + 4, 4), part)
            lhs = jnp.concatenate([tokens[k][:, cols], tokens[4 + k][:, cols]], 0)
            term = jnp.dot(lhs, w[j][...], preferred_element_type=F32)
            total = term if total is None else total + term
        outs[k][0] = total[:rows].astype(BF)
        outs[k][1] = total[rows:].astype(BF)


def partial_values(at, near, far, blocks):
    rows = near[0].shape[0]
    out = [shape((2, rows, blocks[0].shape[1]), BF)] * 4
    return call(values_kernel, out, **small(12))(at, *near, *far, *blocks)


def gathered_kernel(m0, m1, m2, m3, own, give, far_keep, far_give):
    rows = own.shape[0]
    for z in range(2):
        total = (m0[z].astype(F32) + m1[z].astype(F32)) + (m2[z].astype(F32) + m3[z].astype(F32))
        if z == 0:
            own[...] = total[:rows]
            give[...] = total[rows:].astype(BF)
        else:
            far_keep[...] = total[:rows].astype(BF)
            far_give[...] = total[rows:].astype(BF)


def turn_over_kernel(at, *refs):
    tokens, cs, out = refs[:8], refs[8:12], refs[12]
    rows = tokens[0].shape[0]
    head = cs[0].shape[2] // 4
    for k in range(4):
        for z in range(2):
            add = []
            for i in range(4):
                which = jnp.where(at[3] == 0, at[1], i)
                c = cs[k][z, :, wide(which, head)].astype(F32)
                add += [c, c]
            x = tokens[z * 4 + k][...].astype(F32) + jnp.concatenate(add, 1)
            begin = (k * 2 + z) * rows
            out[:, begin : begin + rows] = x.astype(BF).T


def turn_over(at, near, far, cs):
    rows, span = near[0].shape
    return call(turn_over_kernel, shape((span, 8 * rows), BF), **small(12))(at, *near, *far, *cs)


def short_kernel(q0, q1, q2, q3, out):
    total = (q0[...].astype(F32) + q1[...].astype(F32)) + (q2[...].astype(F32) + q3[...].astype(F32))
    out[...] = total.astype(BF)


def square_kernel(at, n0, n1, n2, n3, out):
    quarter = n0.shape[2]
    zl, g, h, core = (at[i] for i in range(4))
    for j, n in enumerate((n0, n1, n2, n3)):
        for k in range(4):
            for z in range(2):
                there = zl if z == 0 else 1 - zl
                at_row = place(core, there, lax.rem(g - k + 4, 4), lax.rem(h - j + 4, 4))
                out[wide(at_row, quarter), :] = n[k, z]


def scale_of(sums, spread, repeat, width):
    mean = jnp.sum(spread, -1, keepdims=True) + jnp.sum(sums * sums, -1, keepdims=True) * (1.0 / repeat)
    return lax.rsqrt(mean * (1.0 / width) + epsilon)


def by_layer(core, layer, own, other, acc, v, dims):
    @pl.when(core == layer)
    def _():
        acc[...] = lax.dot_general(v, own[...], (dims, ((), ())), preferred_element_type=F32)

    @pl.when(core != layer)
    def _():
        acc[...] = lax.dot_general(v, other[...], (dims, ((), ())), preferred_element_type=F32)

    return acc[...]


AHEAD = ((1,), (0,))
BEHIND = ((1,), (1,))


def first_kernel(repeat, width, at, own, other, mine, theirs, far_mine, far_theirs, y0, spread, u, c_out, acc):
    one = mine[...] + far_mine[...].astype(F32)
    two = theirs[...].astype(F32) + far_theirs[...].astype(F32)
    u[0] = jnp.where(at[3] == 0, one, two)
    u[1] = jnp.where(at[3] == 0, two, one)
    c = scale_of(y0[...], spread[...], repeat, width) * u[0]
    sums = y0[...] + repeat * c
    value = u[1] + by_layer(at[3], 1, own, other, acc, c.astype(BF), AHEAD)
    c_out[...] = (c + scale_of(sums, spread[...], repeat, width) * value).astype(BF)


def lower_of(width, at, layer, own, other, acc, g, sums, sigma, value):
    vg = g.astype(BF)
    du = by_layer(at[3], layer, own, other, acc, vg, BEHIND)
    dot = jnp.sum(vg.astype(F32) * value, -1, keepdims=True) * (1.0 / width)
    return g + sigma * du - sigma * sigma * dot * sums


def pick(at, a, b):
    first = at[3] == 0
    return jnp.where(first, a, b), jnp.where(first, b, a)


def turn_kernel(
    repeat, width, at, own, other, u, y0, spread, c_in, g4,
    value, sums, sigma, keep, give, far_keep, far_give, g_out, acc,
):
    c = c_in[...]
    base = c.astype(F32)
    inputs = []
    for layer in range(2):
        inputs.append(base)
        sums[layer] = y0[...] + repeat * base
        s = scale_of(sums[layer], spread[...], repeat, width)
        sigma[layer] = jnp.broadcast_to(s, sigma.shape[1:])
        value[layer] = s * (u[layer] + by_layer(at[3], layer, own, other, acc, c, AHEAD))
        base = base + value[layer]
        c = base.astype(BF)
    half = keep.shape[1]
    mine, theirs = pick(at, *inputs)
    low = at[0] == 0
    for c, here, there in ((mine, keep, far_keep), (theirs, give, far_give)):
        c = c.astype(BF).astype(F32)
        here[...] = jnp.where(low, c[:, :half], c[:, half:]).astype(BF)
        there[...] = jnp.where(low, c[:, half:], c[:, :half]).astype(BF)
    g = g4[...]
    for layer in (1, 0):
        g = lower_of(width, at, layer, own, other, acc, g, sums[layer], sigma[layer][:, :1], value[layer])
    g_out[...] = g.astype(BF)


def send_kernel(width, at, own, other, g4, g_in, value, sums, sigma, keep, give, acc):
    g = jnp.where(at[4] == 1, g4[...], g_in[...].astype(F32))
    out = [None, None]
    for layer in (1, 0):
        s = sigma[layer][:, :1]
        out[layer] = g.astype(BF).astype(F32) * s
        if layer == 1:
            g = lower_of(width, at, 1, own, other, acc, g, sums[1], s, value[1])
    mine, theirs = pick(at, *out)
    keep[...] = mine.astype(BF)
    give[...] = theirs.astype(BF)


def chain_call(kernel, out, at, *args):
    rows, kv = args[2].shape[-2:]
    return call(
        kernel,
        out,
        in_specs=[pl.BlockSpec(memory_space=pltpu.SMEM)] + [pl.BlockSpec(memory_space=pltpu.VMEM)] * len(args),
        scratch_shapes=[pltpu.VMEM((rows, kv), F32)],
    )(at, *args)


def wgrad_kernel(at, turned, r0, r1, r2, r3, *outs):
    right = jnp.concatenate([r[z] for r in (r0, r1, r2, r3) for z in range(2)], 0)
    part = outs[0].shape[0]
    for j in range(4):
        rows = wide(lax.rem(at[2] + j, 4), part)
        outs[j][...] = jnp.dot(turned[rows, :], right, preferred_element_type=F32).astype(BF)


AXES = ("zh", "co", "zl", "y", "x")


def move(v, where):
    flat = lambda d: (((d[0] * 2 + d[1]) * 2 + d[2]) * 4 + d[3] % 4) * 4 + d[4] % 4
    every = [(a, b, c, d, e) for a in range(2) for b in range(2) for c in range(2) for d in range(4) for e in range(4)]
    pairs = [(flat(d), flat(where(*d))) for d in every if where(*d) is not None]
    return lax.ppermute(v, AXES, pairs)


def ring(v, k, on_y):
    if k % 4 == 0:
        return v
    return move(v, lambda a, b, c, y, x: (a, b, c, y + k, x) if b == on_y else (a, b, c, y, x + k))


def to_g(v, k):
    return ring(v, k, 0)


def to_h(v, k):
    return ring(v, k, 1)


def along_x(v, k):
    return v if k == 0 else move(v, lambda a, b, c, y, x: (a, b, c, y, x + k))


def to_z(v):
    return move(v, lambda a, b, c, y, x: (a, b, 1 - c, y, x))


def to_core(v):
    return move(v, lambda a, b, c, y, x: (a, 1 - b, c, y, x))


def to_z_core(v):
    return move(v, lambda a, b, c, y, x: (a, 1 - b, 1 - c, y, x))


def up(v):
    return move(v, lambda a, b, c, y, x: (1, b, c, y, x) if a == 0 else None)


def down(v):
    return move(v, lambda a, b, c, y, x: (0, b, c, y, x) if a == 1 else None)


def per_device(value_weight, norm_gain, mask_logits, gumbel_noise, stream_in, stream_grad):
    zh, co, zl, y, x = (lax.axis_index(n) for n in AXES)
    _, rows, width = stream_in.shape
    kv = value_weight.shape[2]
    head = kv // VHEADS
    repeat = width // kv
    part = value_weight.shape[1]
    own = zl * 16 + y * 4 + x
    first = co == 0
    at = jnp.stack([zl, jnp.where(first, y, x), jnp.where(first, x, y), co, zh])
    weight = value_weight[0]
    gain = lax.dynamic_slice_in_dim(norm_gain[0].astype(F32), own * part, part, 0)[:, None]
    wide32 = shape((rows, kv), F32)
    half = shape((rows, kv), BF)

    near, far = token_blocks(at, stream_in)
    far = to_z(far)
    near = [to_g(near[k], k) for k in range(4)]
    scaled, *quarters = masked_weights(x.reshape(1), mask_logits[0], gumbel_noise[0], weight, gain)
    quarters = [along_x(quarters[k], k) for k in range(4)]
    blocks = [to_h(scaled, k) for k in range(4)]
    swapped = to_core(far)
    far = pair_blocks(at, far, swapped)
    far = [to_g(far[k], k) for k in range(4)]

    short = call(short_kernel, shape(quarters[0].shape, BF))(*quarters)
    short = jnp.stack([short, to_z(short)])
    short = jnp.stack([to_g(short, k) for k in range(4)])
    square = [to_h(short, k) for k in range(4)]
    n = call(square_kernel, shape((kv, kv), BF), **small(4))(at, *square)
    n_other = to_core(n)

    u = partial_values(at, near, far, blocks)
    u = [to_g(u[k], -k) for k in range(4)]
    mine, give, far_keep, far_give = call(gathered_kernel, (wide32, half, half, half))(*u)
    far_mine = to_z(far_keep)
    far_theirs = to_z_core(far_give)
    theirs = to_core(give)
    y0, spread, g4 = token_sums(at[3:4], stream_in, stream_grad, head)

    two = shape((2, rows, kv), F32)
    u, c = chain_call(
        functools.partial(first_kernel, repeat, width),
        (two, half),
        at, n, n_other, mine, theirs, far_mine, far_theirs, y0, spread,
    )
    c_in = up(c)
    quarter = shape((rows, kv // 2), BF)
    value, sums, sigma, keep, give, far_keep, far_give, g = chain_call(
        functools.partial(turn_kernel, repeat, width),
        (two, two, shape((2, rows, head), F32)) + (quarter,) * 4 + (half,),
        at, n, n_other, u, y0, spread, c_in, g4,
    )
    g_in = down(g)
    cs = jnp.stack([
        jnp.concatenate([keep, to_core(give)]), jnp.concatenate([to_z(far_keep), to_z_core(far_give)])
    ])
    cs = [to_g(cs, k) for k in range(4)]
    keep, give = chain_call(
        functools.partial(send_kernel, width), (half, half),
        at, n, n_other, g4, g_in, value, sums, sigma,
    )
    right = jnp.stack([jnp.concatenate([keep, to_core(give)]), jnp.concatenate([to_z(keep), to_z_core(give)])])
    right = [to_g(right, k) for k in range(4)]
    turned = turn_over(at, near, far, cs)
    term = call(wgrad_kernel, [shape((part, kv), BF)] * 4, **small(5))(at, turned, *right)
    term = [to_h(term[k], k) for k in range(4)]
    return logit_gradient(mask_logits[0], gumbel_noise[0], weight, gain, term)[None]


def solution(mesh):
    fine = Mesh(mesh.devices.reshape(2, 2, 2, 4, 4), ("zh", "co", "zl", "y", "x"))
    dp = ("zl", "y", "x")

    return jax.shard_map(
        per_device,
        mesh=fine,
        in_specs=(
            P(LAYER, dp, None),
            P(LAYER, None),
            P(LAYER, None, dp, None),
            P(LAYER, None, dp, None),
            P(None, dp, None),
            P(None, dp, None),
        ),
        out_specs=P(LAYER, None, dp, None),
        check_vma=False,
    )
```

```python
import functools

import jax
import jax.numpy as jnp
from jax import lax
from jax.experimental import pallas as pl
from jax.experimental.pallas import tpu as pltpu
from jax.sharding import Mesh
from jax.sharding import PartitionSpec as P


VHEADS = 8
sharpness_divisor = 0.6666667
epsilon = 1e-05
BF = jnp.bfloat16
F32 = jnp.float32
INTERPRET = False
HBM = pltpu.HBM
KEEPS = ((0, 1), (0, 2), (0, 3), (1, 2), (1, 3), (2, 3))
LAYER = ("zh", "co")


def shape(dims, dtype):
    return jax.ShapeDtypeStruct(dims, dtype)


def call(kernel, out, **rest):
    params = pltpu.CompilerParams(vmem_limit_bytes=20 << 20)
    return pl.pallas_call(kernel, out_shape=out, interpret=INTERPRET, compiler_params=params, **rest)


def tiles(width, most=128):
    step = min(width, most)
    return [slice(i, i + step) for i in range(0, width, step)]


def by_tile(rows, width, most=128):
    cols = tiles(width, min(most, 128))
    return pltpu.VMEM((len(cols), rows, cols[0].stop), F32)


def pattern_probs(logits, noise, s):
    expo = [
        jnp.exp((logits[k, :, s].astype(F32) + noise[k, :, s].astype(F32)) * (1.0 / sharpness_divisor))
        for k in range(6)
    ]
    inverse = 1.0 / (((expo[0] + expo[1]) + (expo[2] + expo[3])) + (expo[4] + expo[5]))
    return [e * inverse for e in expo]


def mask_kernel(at, logits, noise, weight, gain, scaled, q0, q1, q2, q3, rows):
    for i, s in enumerate(tiles(weight.shape[1])):
        p = pattern_probs(logits, noise, s)
        for r in range(4):
            kept = [p[k] for k in range(6) if r in KEEPS[k]]
            rows.at[i][pl.ds(r, kept[0].shape[0], stride=4), :] = kept[0] + kept[1] + kept[2]
        value = weight[:, s].astype(F32) * rows[i] * gain[...]
        scaled[:, s] = value.astype(BF)
        rows[i] = value
        quarter = q0.shape[0]
        for k, q in enumerate((q0, q1, q2, q3)):
            begin = pl.multiple_of(lax.rem(at[0] + k, 4) * quarter, quarter)
            one = rows.at[i][pl.ds(begin, quarter), :]
            two = rows.at[i][pl.ds(begin + 4 * quarter, quarter), :]
            q[:, s] = (one + two).astype(BF)


def masked_weights(at, logits, noise, weight, gain):
    n, kv = weight.shape
    return call(
        mask_kernel,
        (shape((n, kv), BF),) + (shape((n // 8, kv), BF),) * 4,
        in_specs=[pl.BlockSpec(memory_space=pltpu.SMEM)] + [pl.BlockSpec(memory_space=pltpu.VMEM)] * 4,
        scratch_shapes=[by_tile(n, kv)],
    )(at, logits, noise, weight, gain)


def final_kernel(logits, noise, weight, gain, *refs):
    parts, out, rows = refs[:-2], refs[-2], refs[-1]
    tile = rows.shape[2]
    where = [(j, at) for j in range(len(parts) // 4) for at in range(0, parts[j * 4].shape[1], tile)]
    for i, (j, at) in enumerate(where):
        s, inner = slice(i * tile, (i + 1) * tile), slice(at, at + tile)
        mine = parts[j * 4 : j * 4 + 4]
        total = (mine[0][:, inner].astype(F32) + mine[1][:, inner].astype(F32)) + (
            mine[2][:, inner].astype(F32) + mine[3][:, inner].astype(F32)
        )
        rows[i] = total * gain[...] * weight[:, s].astype(F32) * (1.0 / sharpness_divisor)
        d = [rows.at[i][pl.ds(r, logits.shape[1], stride=4), :] for r in range(4)]
        p = pattern_probs(logits, noise, s)
        dprob = [d[a] + d[b] for a, b in KEEPS]
        mean = p[0] * dprob[0]
        for k in range(1, 6):
            mean = mean + p[k] * dprob[k]
        for k in range(6):
            out[k, :, s] = (p[k] * (dprob[k] - mean)).astype(BF)


def logit_gradient(logits, noise, weight, gain, parts):
    return call(
        final_kernel,
        shape(logits.shape, BF),
        scratch_shapes=[by_tile(*weight.shape, most=weight.shape[1] // 8)],
    )(logits, noise, weight, gain, *parts)


def run_copies(copies, sems):
    copies = [pltpu.make_async_copy(src, dst, sems.at[i]) for i, (src, dst) in enumerate(copies)]
    for copy in copies:
        copy.start()
    for copy in copies:
        copy.wait()


def wide(index, part):
    return pl.ds(pl.multiple_of(index * part, part), part)


def place(core, zl, g, h):
    return zl * 16 + jnp.where(core == 0, g * 4 + h, h * 4 + g)


def slice_kernel(at, tokens, out, sem):
    width = out.shape[1]
    source = wide(1 - at[0], width)
    copy = pltpu.make_async_copy(tokens.at[at[3], :, source], out, sem)
    copy.start()
    copy.wait()


def far_half(at, tokens):
    rows, width = tokens.shape[1:]
    return call(
        slice_kernel,
        shape((rows, width // 2), BF),
        in_specs=[pl.BlockSpec(memory_space=pltpu.SMEM), pl.BlockSpec(memory_space=HBM)],
        out_specs=pl.BlockSpec(memory_space=pltpu.VMEM),
        scratch_shapes=[pltpu.SemaphoreType.DMA],
    )(at, tokens)


def blocks_kernel(at, tokens, mine, other, o0, o1, o2, o3, sems):
    zl, g, core = at[0], at[1], at[3]
    rows, width = tokens.shape[1:]
    part = width // 32
    copies = []
    for k, out in enumerate((o0, o1, o2, o3)):
        for i in range(4):
            near = wide(place(core, zl, lax.rem(g + k, 4), i), part)
            far = wide(place(core, 0, lax.rem(g + k, 4), i), part)
            sources = (tokens.at[core, :, near], tokens.at[1 - core, :, near], mine.at[:, far], other.at[:, far])
            for r, source in enumerate(sources):
                copies.append((source, out.at[pl.ds(r * rows, rows), pl.ds(i * part, part)]))
    run_copies(copies, sems)


def token_blocks(at, tokens, mine, other):
    rows, width = tokens.shape[1:]
    block = pl.BlockSpec(memory_space=pl.ANY)
    return call(
        blocks_kernel,
        (shape((4 * rows, width // 8), BF),) * 4,
        in_specs=[pl.BlockSpec(memory_space=pltpu.SMEM), pl.BlockSpec(memory_space=HBM), block, block],
        out_specs=(block,) * 4,
        scratch_shapes=[pltpu.SemaphoreType.DMA((64,))],
    )(at, tokens, mine, other)


def sums_kernel(repeat, head, core, tokens, grads, y0, spread, g4):
    t = tokens[0]
    pieces = [t[:, r * head : (r + 1) * head].astype(F32) for r in range(repeat)]
    total = functools.reduce(lambda a, b: a + b, pieces)
    mean = total * (1.0 / repeat)
    squares = functools.reduce(lambda a, b: a + b, [(p - mean) * (p - mean) for p in pieces])
    y0[...] = total

    @pl.when(pl.program_id(0) == 0)
    def _():
        spread[...] = squares

    @pl.when(pl.program_id(0) != 0)
    def _():
        spread[...] += squares

    g = grads[0]
    g4[...] = functools.reduce(
        lambda a, b: a + b, [g[:, r * head : (r + 1) * head].astype(F32) for r in range(repeat)]
    )


def token_sums(core, tokens, grads, head):
    rows, width = tokens.shape[1:]
    span = width // VHEADS
    block = pl.BlockSpec((1, rows, span), lambda h, core: (core[0], 0, h))
    narrow = pl.BlockSpec((rows, head), lambda h, core: (0, h))
    return call(
        functools.partial(sums_kernel, span // head, head),
        (
            shape((rows, VHEADS * head), F32),
            shape((rows, head), F32),
            shape((rows, VHEADS * head), F32),
        ),
        grid_spec=pltpu.PrefetchScalarGridSpec(
            num_scalar_prefetch=1,
            grid=(VHEADS,),
            in_specs=[block, block],
            out_specs=(
                narrow,
                pl.BlockSpec((rows, head), lambda h, core: (0, 0)),
                narrow,
            ),
        ),
    )(core, tokens, grads)


def small(count):
    vmem = pl.BlockSpec(memory_space=pltpu.VMEM)
    return dict(in_specs=[pl.BlockSpec(memory_space=pltpu.SMEM)] + [vmem] * count)


def values_kernel(far, at, *refs):
    tokens, w, outs = refs[:4], refs[4:8], refs[8:]
    part = w[0].shape[0]
    rows = outs[0].shape[0]
    mine = slice(rows, 2 * rows) if far else slice(0, rows)
    for k in range(0, 4, 2):
        total = None
        for j in range(4):
            cols = wide(lax.rem(at[2] - j + 4, 4), part)
            lhs = jnp.concatenate([tokens[k][mine, cols], tokens[k + 1][mine, cols]], 0)
            term = jnp.dot(lhs, w[j][...], preferred_element_type=F32)
            total = term if total is None else total + term
        outs[k][...] = total[:rows].astype(BF)
        outs[k + 1][...] = total[rows:].astype(BF)


def partial_values(at, tokens, blocks, far):
    out = [shape((tokens[0].shape[0] // 2, blocks[0].shape[1]), BF)] * 4
    return call(functools.partial(values_kernel, far), out, **small(8))(at, *tokens, *blocks)


def gathered_kernel(m0, m1, m2, m3, keep, give):
    rows = keep.shape[0]
    for i, out in enumerate((keep, give)):
        p = [m[i * rows : (i + 1) * rows, :].astype(F32) for m in (m0, m1, m2, m3)]
        out[...] = ((p[0] + p[1]) + (p[2] + p[3])).astype(out.dtype)


def turn_over_kernel(at, *refs):
    tokens, cs, out = refs[:4], refs[4:8], refs[8]
    rows = tokens[0].shape[0] // 2
    head = cs[0].shape[2] // 4
    for k in range(4):
        for z in range(2):
            add = []
            for i in range(4):
                which = jnp.where(at[3] == 0, at[1], i)
                c = cs[k][z, :, wide(which, head)].astype(F32)
                add += [c, c]
            x = tokens[k][z * rows : (z + 1) * rows, :].astype(F32) + jnp.concatenate(add, 1)
            begin = (k * 2 + z) * rows
            out[:, begin : begin + rows] = x.astype(BF).T


def turn_over(at, tokens, cs):
    rows, span = tokens[0].shape
    return call(turn_over_kernel, shape((span, 4 * rows), BF), **small(8))(at, *tokens, *cs)


def short_kernel(q0, q1, q2, q3, out):
    total = (q0[...].astype(F32) + q1[...].astype(F32)) + (q2[...].astype(F32) + q3[...].astype(F32))
    out[...] = total.astype(BF)


def square_kernel(swapped, at, n0, n1, n2, n3, out):
    quarter = n0.shape[2]
    zl, g, h, core = (at[i] for i in range(4))
    if swapped:
        g, h, core = h, g, 1 - core
    for j, n in enumerate((n0, n1, n2, n3)):
        for k in range(4):
            for z in range(2):
                there = zl if z == 0 else 1 - zl
                at_row = place(core, there, lax.rem(g - k + 4, 4), lax.rem(h - j + 4, 4))
                out[wide(at_row, quarter), :] = n[k, z]


def scale_of(sums, spread, repeat, width):
    mean = jnp.sum(spread, -1, keepdims=True) + jnp.sum(sums * sums, -1, keepdims=True) * (1.0 / repeat)
    return lax.rsqrt(mean * (1.0 / width) + epsilon)


def by_layer(core, layer, own, other, acc, v, dims):
    @pl.when(core == layer)
    def _():
        acc[...] = lax.dot_general(v, own[...], (dims, ((), ())), preferred_element_type=F32)

    @pl.when(core != layer)
    def _():
        acc[...] = lax.dot_general(v, other[...], (dims, ((), ())), preferred_element_type=F32)

    return acc[...]


AHEAD = ((1,), (0,))
BEHIND = ((1,), (1,))


def first_kernel(repeat, width, at, own, other, mine, theirs, far_mine, far_theirs, y0, spread, u, c_out, acc):
    one = mine[...] + far_mine[...].astype(F32)
    two = theirs[...].astype(F32) + far_theirs[...].astype(F32)
    u[0] = jnp.where(at[3] == 0, one, two)
    u[1] = jnp.where(at[3] == 0, two, one)
    c = scale_of(y0[...], spread[...], repeat, width) * u[0]
    sums = y0[...] + repeat * c
    value = u[1] + by_layer(at[3], 1, own, other, acc, c.astype(BF), AHEAD)
    c_out[...] = (c + scale_of(sums, spread[...], repeat, width) * value).astype(BF)


def lower_of(width, at, layer, own, other, acc, g, sums, sigma, value):
    vg = g.astype(BF)
    du = by_layer(at[3], layer, own, other, acc, vg, BEHIND)
    dot = jnp.sum(vg.astype(F32) * value, -1, keepdims=True) * (1.0 / width)
    return g + sigma * du - sigma * sigma * dot * sums


def pick(at, a, b):
    first = at[3] == 0
    return jnp.where(first, a, b), jnp.where(first, b, a)


def turn_kernel(
    repeat, width, at, own, other, u, y0, spread, c_in, g4,
    value, sums, sigma, keep, give, far_keep, far_give, g_out, acc,
):
    c = c_in[...]
    base = c.astype(F32)
    inputs = []
    for layer in range(2):
        inputs.append(base)
        sums[layer] = y0[...] + repeat * base
        s = scale_of(sums[layer], spread[...], repeat, width)
        sigma[layer] = jnp.broadcast_to(s, sigma.shape[1:])
        value[layer] = s * (u[layer] + by_layer(at[3], layer, own, other, acc, c, AHEAD))
        base = base + value[layer]
        c = base.astype(BF)
    half = keep.shape[1]
    mine, theirs = pick(at, *inputs)
    low = at[0] == 0
    for c, here, there in ((mine, keep, far_keep), (theirs, give, far_give)):
        c = c.astype(BF).astype(F32)
        here[...] = jnp.where(low, c[:, :half], c[:, half:]).astype(BF)
        there[...] = jnp.where(low, c[:, half:], c[:, :half]).astype(BF)
    g = g4[...]
    for layer in (1, 0):
        g = lower_of(width, at, layer, own, other, acc, g, sums[layer], sigma[layer][:, :1], value[layer])
    g_out[...] = g.astype(BF)


def send_kernel(width, at, own, other, g4, g_in, value, sums, sigma, keep, give, acc):
    g = jnp.where(at[4] == 1, g4[...], g_in[...].astype(F32))
    out = [None, None]
    for layer in (1, 0):
        s = sigma[layer][:, :1]
        out[layer] = g.astype(BF).astype(F32) * s
        if layer == 1:
            g = lower_of(width, at, 1, own, other, acc, g, sums[1], s, value[1])
    mine, theirs = pick(at, *out)
    keep[...] = mine.astype(BF)
    give[...] = theirs.astype(BF)


def chain_call(kernel, out, at, *args):
    rows, kv = args[2].shape[-2:]
    return call(
        kernel,
        out,
        in_specs=[pl.BlockSpec(memory_space=pltpu.SMEM)] + [pl.BlockSpec(memory_space=pltpu.VMEM)] * len(args),
        scratch_shapes=[pltpu.VMEM((rows, kv), F32)],
    )(at, *args)


def wgrad_first_kernel(at, turned, *refs):
    near, far, out, right = refs[:4], refs[4:8], refs[8], refs[9]
    for k in range(4):
        for z, r in enumerate((near[k], far[k])):
            begin = (k * 2 + z) * r.shape[0]
            right[begin : begin + r.shape[0], :] = r[...]
    wgrad_kernel((2,), at, turned, right, out)


def wgrad_kernel(ahead, at, turned, right, *outs):
    part = outs[0].shape[0]
    for j, out in zip(ahead, outs):
        rows = wide(lax.rem(at[2] + j, 4), part)
        out[...] = jnp.dot(turned[rows, :], right[...], preferred_element_type=F32).astype(BF)


AXES = ("zh", "co", "zl", "y", "x")


def move(v, where):
    flat = lambda d: (((d[0] * 2 + d[1]) * 2 + d[2]) * 4 + d[3] % 4) * 4 + d[4] % 4
    every = [(a, b, c, d, e) for a in range(2) for b in range(2) for c in range(2) for d in range(4) for e in range(4)]
    pairs = [(flat(d), flat(where(*d))) for d in every if where(*d) is not None]
    return lax.ppermute(v, AXES, pairs)


def ring(v, k, on_y):
    if k % 4 == 0:
        return v
    return move(v, lambda a, b, c, y, x: (a, b, c, y + k, x) if b == on_y else (a, b, c, y, x + k))


def to_g(v, k):
    return ring(v, k, 0)


def to_h(v, k):
    return ring(v, k, 1)


def ring_all(vs, way):
    return [vs[0] if k == 0 else to_g(vs[k], way * k) for k in range(4)]


def along_x(v, k):
    return v if k == 0 else move(v, lambda a, b, c, y, x: (a, b, c, y, x + k))


def to_z(v):
    return move(v, lambda a, b, c, y, x: (a, b, 1 - c, y, x))


def to_core(v):
    return move(v, lambda a, b, c, y, x: (a, 1 - b, c, y, x))


def to_z_core(v):
    return move(v, lambda a, b, c, y, x: (a, 1 - b, 1 - c, y, x))


def up(v):
    return move(v, lambda a, b, c, y, x: (1, b, c, y, x) if a == 0 else None)


def down(v):
    return move(v, lambda a, b, c, y, x: (0, b, c, y, x) if a == 1 else None)


def per_device(value_weight, norm_gain, mask_logits, gumbel_noise, stream_in, stream_grad):
    zh, co, zl, y, x = (lax.axis_index(n) for n in AXES)
    _, rows, width = stream_in.shape
    kv = value_weight.shape[2]
    head = kv // VHEADS
    repeat = width // kv
    part = value_weight.shape[1]
    own = zl * 16 + y * 4 + x
    first = co == 0
    at = jnp.stack([zl, jnp.where(first, y, x), jnp.where(first, x, y), co, zh])
    weight = value_weight[0]
    gain = lax.dynamic_slice_in_dim(norm_gain[0].astype(F32), own * part, part, 0)[:, None]
    wide32 = shape((rows, kv), F32)
    half = shape((rows, kv), BF)

    stream = stream_in if INTERPRET else pltpu.with_memory_space_constraint(stream_in, HBM)
    far = far_half(at, stream)
    far = to_z(far)
    scaled, *quarters = masked_weights(x.reshape(1), mask_logits[0], gumbel_noise[0], weight, gain)
    blocks = [to_h(scaled, k) for k in range(4)]
    quarters = [along_x(quarters[k], k) for k in range(4)]
    swapped = to_core(far)
    tokens = token_blocks(at, stream, far, swapped)
    tokens = [to_g(tokens[k], k) for k in range(4)]
    short = call(short_kernel, shape(quarters[0].shape, BF))(*quarters)
    short = jnp.stack([short, to_z(short)])
    short = jnp.stack([to_g(short, k) for k in range(4)])
    square = [to_h(short, k) for k in range(4)]
    swapped = [to_core(v) for v in square]
    n = call(functools.partial(square_kernel, 0), shape((kv, kv), BF), **small(4))(at, *square)
    n_other = call(functools.partial(square_kernel, 1), shape((kv, kv), BF), **small(4))(at, *swapped)

    u_far = partial_values(at, tokens, blocks, True)
    u_far = ring_all(u_far, -1)
    u_near = partial_values(at, tokens, blocks, False)
    u_near = ring_all(u_near, -1)
    far_keep, far_give = call(gathered_kernel, (half, half))(*u_far)
    far_mine = to_z(far_keep)
    far_theirs = to_z_core(far_give)
    mine, give = call(gathered_kernel, (wide32, half))(*u_near)
    theirs = to_core(give)
    y0, spread, g4 = token_sums(at[3:4], stream_in, stream_grad, head)

    two = shape((2, rows, kv), F32)
    u, c = chain_call(
        functools.partial(first_kernel, repeat, width),
        (two, half),
        at, n, n_other, mine, theirs, far_mine, far_theirs, y0, spread,
    )
    c_in = up(c)
    quarter = shape((rows, kv // 2), BF)
    value, sums, sigma, keep, give, far_keep, far_give, g = chain_call(
        functools.partial(turn_kernel, repeat, width),
        (two, two, shape((2, rows, head), F32)) + (quarter,) * 4 + (half,),
        at, n, n_other, u, y0, spread, c_in, g4,
    )
    g_in = down(g)
    cs = jnp.stack([
        jnp.concatenate([keep, to_core(give)]), jnp.concatenate([to_z(far_keep), to_z_core(far_give)])
    ])
    cs = [to_g(cs, k) for k in range(4)]
    keep, give = chain_call(
        functools.partial(send_kernel, width), (half, half),
        at, n, n_other, g4, g_in, value, sums, sigma,
    )
    near = to_core(give)
    far, far_give = to_z(keep), to_z_core(give)
    near = ring_all([jnp.concatenate([keep, near])] * 4, 1)
    far = ring_all([jnp.concatenate([far, far_give])] * 4, 1)
    turned = turn_over(at, tokens, cs)
    block = shape((part, kv), BF)
    t2, right = call(wgrad_first_kernel, [block, shape(turned.shape, BF)], **small(9))(at, turned, *near, *far)
    t2 = to_h(t2, 2)
    t1, t3 = call(functools.partial(wgrad_kernel, (1, 3)), [block] * 2, **small(2))(at, turned, right)
    t1, t3 = to_h(t1, 1), to_h(t3, 3)
    (t0,) = call(functools.partial(wgrad_kernel, (0,)), [block], **small(2))(at, turned, right)
    return logit_gradient(mask_logits[0], gumbel_noise[0], weight, gain, [t0, t1, t2, t3])[None]


def solution(mesh):
    fine = Mesh(mesh.devices.reshape(2, 2, 2, 4, 4), ("zh", "co", "zl", "y", "x"))
    dp = ("zl", "y", "x")

    return jax.shard_map(
        per_device,
        mesh=fine,
        in_specs=(
            P(LAYER, dp, None),
            P(LAYER, None),
            P(LAYER, None, dp, None),
            P(LAYER, None, dp, None),
            P(None, dp, None),
            P(None, dp, None),
        ),
        out_specs=P(LAYER, None, dp, None),
        check_vma=False,
    )
```

```python
import functools

import jax
import jax.numpy as jnp
from jax import lax
from jax.experimental import pallas as pl
from jax.experimental.pallas import tpu as pltpu
from jax.sharding import Mesh
from jax.sharding import PartitionSpec as P


VHEADS = 8
sharpness_divisor = 0.6666667
epsilon = 1e-05
BF = jnp.bfloat16
F32 = jnp.float32
INTERPRET = False
HBM = pltpu.HBM
KEEPS = ((0, 1), (0, 2), (0, 3), (1, 2), (1, 3), (2, 3))
LAYER = ("zh", "co")


def shape(dims, dtype):
    return jax.ShapeDtypeStruct(dims, dtype)


def call(kernel, out, **rest):
    params = pltpu.CompilerParams(vmem_limit_bytes=20 << 20)
    return pl.pallas_call(kernel, out_shape=out, interpret=INTERPRET, compiler_params=params, **rest)


def tiles(width, most=128):
    step = min(width, most)
    return [slice(i, i + step) for i in range(0, width, step)]


def by_tile(rows, width, most=128):
    cols = tiles(width, min(most, 128))
    return pltpu.VMEM((len(cols), rows, cols[0].stop), F32)


def pattern_probs(logits, noise, s):
    expo = [
        jnp.exp((logits[k, :, s].astype(F32) + noise[k, :, s].astype(F32)) * (1.0 / sharpness_divisor))
        for k in range(6)
    ]
    inverse = 1.0 / (((expo[0] + expo[1]) + (expo[2] + expo[3])) + (expo[4] + expo[5]))
    return [e * inverse for e in expo]


def gain_column(index, gain, rows):
    row = gain[:, pl.ds(pl.multiple_of(index * rows, rows), rows)].astype(F32)
    return jnp.broadcast_to(row, (8, rows)).T[:, :1]


def mask_kernel(at, logits, noise, weight, gain, scaled, q0, q1, q2, q3, rows):
    column = gain_column(at[1], gain, weight.shape[0])
    for i, s in enumerate(tiles(weight.shape[1])):
        p = pattern_probs(logits, noise, s)
        for r in range(4):
            kept = [p[k] for k in range(6) if r in KEEPS[k]]
            rows.at[i][pl.ds(r, kept[0].shape[0], stride=4), :] = kept[0] + kept[1] + kept[2]
        value = weight[:, s].astype(F32) * rows[i] * column
        scaled[:, s] = value.astype(BF)
        rows[i] = value
        quarter = q0.shape[0]
        for k, q in enumerate((q0, q1, q2, q3)):
            begin = pl.multiple_of(lax.rem(at[0] + k, 4) * quarter, quarter)
            one = rows.at[i][pl.ds(begin, quarter), :]
            two = rows.at[i][pl.ds(begin + 4 * quarter, quarter), :]
            q[:, s] = (one + two).astype(BF)


def masked_weights(at, logits, noise, weight, gain):
    n, kv = weight.shape
    return call(
        mask_kernel,
        (shape((n, kv), BF),) + (shape((n // 8, kv), BF),) * 4,
        in_specs=[pl.BlockSpec(memory_space=pltpu.SMEM)] + [pl.BlockSpec(memory_space=pltpu.VMEM)] * 4,
        scratch_shapes=[by_tile(n, kv)],
    )(at, logits, noise, weight, gain)


def ready_kernel(at, logits, noise, weight, gain, probs, ready):
    column = gain_column(at[1], gain, weight.shape[0]) * (1.0 / sharpness_divisor)
    for s in tiles(weight.shape[1]):
        for k, p in enumerate(pattern_probs(logits, noise, s)):
            probs[k, :, s] = p
        ready[:, s] = weight[:, s].astype(F32) * column


def final_kernel(probs, ready, *refs):
    parts, out, rows, done, sems = refs[:-4], *refs[-4:]
    copies = []
    for i, s in enumerate(tiles(ready.shape[1])):
        total = (parts[0][:, s].astype(F32) + parts[1][:, s].astype(F32)) + (
            parts[2][:, s].astype(F32) + parts[3][:, s].astype(F32)
        )
        rows[i] = total * ready[:, s]
        d = [rows.at[i][pl.ds(r, probs.shape[1], stride=4), :] for r in range(4)]
        p = [probs[k, :, s] for k in range(6)]
        dprob = [d[a] + d[b] for a, b in KEEPS]
        mean = p[0] * dprob[0]
        for k in range(1, 6):
            mean = mean + p[k] * dprob[k]
        for k in range(6):
            done[i, k] = (p[k] * (dprob[k] - mean)).astype(BF)
        copies.append(pltpu.make_async_copy(done.at[i], out.at[:, :, s], sems.at[i]))
        copies[-1].start()
    for copy in copies:
        copy.wait()


def logit_gradient(probs, ready, parts):
    count = len(tiles(ready.shape[1]))
    tile = ready.shape[1] // count
    return call(
        final_kernel,
        shape(probs.shape, BF),
        out_specs=pl.BlockSpec(memory_space=pl.ANY),
        scratch_shapes=[
            by_tile(*ready.shape),
            pltpu.VMEM((count, *probs.shape[:2], tile), BF),
            pltpu.SemaphoreType.DMA((count,)),
        ],
    )(probs, ready, *parts)


def run_copies(copies, sems):
    copies = [pltpu.make_async_copy(src, dst, sems.at[i]) for i, (src, dst) in enumerate(copies)]
    for copy in copies:
        copy.start()
    for copy in copies:
        copy.wait()


def wide(index, part):
    return pl.ds(pl.multiple_of(index * part, part), part)


def place(core, zl, g, h):
    return zl * 16 + jnp.where(core == 0, g * 4 + h, h * 4 + g)


def slice_kernel(at, tokens, out, sem):
    width = out.shape[1]
    source = wide(1 - at[0], width)
    copy = pltpu.make_async_copy(tokens.at[at[3], :, source], out, sem)
    copy.start()
    copy.wait()


def far_half(at, tokens):
    rows, width = tokens.shape[1:]
    return call(
        slice_kernel,
        shape((rows, width // 2), BF),
        in_specs=[pl.BlockSpec(memory_space=pltpu.SMEM), pl.BlockSpec(memory_space=HBM)],
        out_specs=pl.BlockSpec(memory_space=pltpu.VMEM),
        scratch_shapes=[pltpu.SemaphoreType.DMA],
    )(at, tokens)


def blocks_kernel(at, tokens, mine, other, o0, o1, o2, o3, sems):
    zl, g, core = at[0], at[1], at[3]
    rows, width = tokens.shape[1:]
    part = width // 32
    copies = []
    for k, out in enumerate((o0, o1, o2, o3)):
        for i in range(4):
            near = wide(place(core, zl, lax.rem(g + k, 4), i), part)
            far = wide(place(core, 0, lax.rem(g + k, 4), i), part)
            sources = (tokens.at[core, :, near], tokens.at[1 - core, :, near], mine.at[:, far], other.at[:, far])
            for r, source in enumerate(sources):
                copies.append((source, out.at[pl.ds(r * rows, rows), pl.ds(i * part, part)]))
    run_copies(copies, sems)


def token_blocks(at, tokens, mine, other):
    rows, width = tokens.shape[1:]
    block = pl.BlockSpec(memory_space=pl.ANY)
    return call(
        blocks_kernel,
        (shape((4 * rows, width // 8), BF),) * 4,
        in_specs=[pl.BlockSpec(memory_space=pltpu.SMEM), pl.BlockSpec(memory_space=HBM), block, block],
        out_specs=(pl.BlockSpec(memory_space=pltpu.VMEM),) * 4,
        scratch_shapes=[pltpu.SemaphoreType.DMA((64,))],
    )(at, tokens, mine, other)


def sums_kernel(repeat, head, core, tokens, grads, y0, spread, g4):
    t = tokens[0]
    pieces = [t[:, r * head : (r + 1) * head].astype(F32) for r in range(repeat)]
    total = functools.reduce(lambda a, b: a + b, pieces)
    mean = total * (1.0 / repeat)
    squares = functools.reduce(lambda a, b: a + b, [(p - mean) * (p - mean) for p in pieces])
    y0[...] = total

    @pl.when(pl.program_id(0) == 0)
    def _():
        spread[...] = squares

    @pl.when(pl.program_id(0) != 0)
    def _():
        spread[...] += squares

    g = grads[0]
    g4[...] = functools.reduce(
        lambda a, b: a + b, [g[:, r * head : (r + 1) * head].astype(F32) for r in range(repeat)]
    )


def token_sums(core, tokens, grads, head):
    rows, width = tokens.shape[1:]
    span = width // VHEADS
    block = pl.BlockSpec((1, rows, span), lambda h, core: (core[0], 0, h))
    narrow = pl.BlockSpec((rows, head), lambda h, core: (0, h))
    return call(
        functools.partial(sums_kernel, span // head, head),
        (
            shape((rows, VHEADS * head), F32),
            shape((rows, head), F32),
            shape((rows, VHEADS * head), F32),
        ),
        grid_spec=pltpu.PrefetchScalarGridSpec(
            num_scalar_prefetch=1,
            grid=(VHEADS,),
            in_specs=[block, block],
            out_specs=(
                narrow,
                pl.BlockSpec((rows, head), lambda h, core: (0, 0)),
                narrow,
            ),
        ),
    )(core, tokens, grads)


def small(count):
    vmem = pl.BlockSpec(memory_space=pltpu.VMEM)
    return dict(in_specs=[pl.BlockSpec(memory_space=pltpu.SMEM)] + [vmem] * count)


def values_kernel(far, at, *refs):
    tokens, w, outs = refs[:4], refs[4:8], refs[8:]
    part = w[0].shape[0]
    rows = outs[0].shape[0]
    mine = slice(rows, 2 * rows) if far else slice(0, rows)
    for k in range(0, 4, 2):
        total = None
        for j in range(4):
            cols = wide(lax.rem(at[2] - j + 4, 4), part)
            lhs = jnp.concatenate([tokens[k][mine, cols], tokens[k + 1][mine, cols]], 0)
            term = jnp.dot(lhs, w[j][...], preferred_element_type=F32)
            total = term if total is None else total + term
        outs[k][...] = total[:rows].astype(BF)
        outs[k + 1][...] = total[rows:].astype(BF)


def partial_values(at, tokens, blocks, far):
    out = [shape((tokens[0].shape[0] // 2, blocks[0].shape[1]), BF)] * 4
    return call(functools.partial(values_kernel, far), out, **small(8))(at, *tokens, *blocks)


def gathered_kernel(m0, m1, m2, m3, keep, give):
    rows = keep.shape[0]
    for i, out in enumerate((keep, give)):
        p = [m[i * rows : (i + 1) * rows, :].astype(F32) for m in (m0, m1, m2, m3)]
        out[...] = ((p[0] + p[1]) + (p[2] + p[3])).astype(out.dtype)


def turn_over_kernel(at, *refs):
    tokens, cs, out = refs[:4], refs[4:8], refs[8]
    rows = tokens[0].shape[0] // 2
    head = cs[0].shape[2] // 4
    for k in range(4):
        for z in range(2):
            add = []
            for i in range(4):
                which = jnp.where(at[3] == 0, at[1], i)
                c = cs[k][z, :, wide(which, head)].astype(F32)
                add += [c, c]
            x = tokens[k][z * rows : (z + 1) * rows, :].astype(F32) + jnp.concatenate(add, 1)
            begin = (k * 2 + z) * rows
            out[:, begin : begin + rows] = x.astype(BF).T


def turn_over(at, tokens, cs):
    rows, span = tokens[0].shape
    return call(turn_over_kernel, shape((span, 4 * rows), BF), **small(8))(at, *tokens, *cs)


def short_kernel(q0, q1, q2, q3, out):
    total = (q0[...].astype(F32) + q1[...].astype(F32)) + (q2[...].astype(F32) + q3[...].astype(F32))
    out[...] = total.astype(BF)


def square_kernel(swapped, at, n0, n1, n2, n3, out):
    quarter = n0.shape[2]
    zl, g, h, core = (at[i] for i in range(4))
    if swapped:
        g, h, core = h, g, 1 - core
    for j, n in enumerate((n0, n1, n2, n3)):
        for k in range(4):
            for z in range(2):
                there = zl if z == 0 else 1 - zl
                at_row = place(core, there, lax.rem(g - k + 4, 4), lax.rem(h - j + 4, 4))
                out[wide(at_row, quarter), :] = n[k, z]


def scale_of(sums, spread, repeat, width):
    mean = jnp.sum(spread, -1, keepdims=True) + jnp.sum(sums * sums, -1, keepdims=True) * (1.0 / repeat)
    return lax.rsqrt(mean * (1.0 / width) + epsilon)


def by_layer(core, layer, own, other, acc, v, dims):
    @pl.when(core == layer)
    def _():
        acc[...] = lax.dot_general(v, own[...], (dims, ((), ())), preferred_element_type=F32)

    @pl.when(core != layer)
    def _():
        acc[...] = lax.dot_general(v, other[...], (dims, ((), ())), preferred_element_type=F32)

    return acc[...]


AHEAD = ((1,), (0,))
BEHIND = ((1,), (1,))


def first_kernel(repeat, width, at, own, other, mine, theirs, far_mine, far_theirs, y0, spread, u, c_out, acc):
    one = mine[...] + far_mine[...].astype(F32)
    two = theirs[...].astype(F32) + far_theirs[...].astype(F32)
    u[0] = jnp.where(at[3] == 0, one, two)
    u[1] = jnp.where(at[3] == 0, two, one)
    c = scale_of(y0[...], spread[...], repeat, width) * u[0]
    sums = y0[...] + repeat * c
    value = u[1] + by_layer(at[3], 1, own, other, acc, c.astype(BF), AHEAD)
    c_out[...] = (c + scale_of(sums, spread[...], repeat, width) * value).astype(BF)


def lower_of(width, at, layer, own, other, acc, g, sums, sigma, value):
    vg = g.astype(BF)
    du = by_layer(at[3], layer, own, other, acc, vg, BEHIND)
    dot = jnp.sum(vg.astype(F32) * value, -1, keepdims=True) * (1.0 / width)
    return g + sigma * du - sigma * sigma * dot * sums


def pick(at, a, b):
    first = at[3] == 0
    return jnp.where(first, a, b), jnp.where(first, b, a)


def turn_kernel(
    repeat, width, at, own, other, u, y0, spread, c_in, g4,
    value, sums, sigma, keep, give, far_keep, far_give, g_out, acc,
):
    c = c_in[...]
    base = c.astype(F32)
    inputs = []
    for layer in range(2):
        inputs.append(base)
        sums[layer] = y0[...] + repeat * base
        s = scale_of(sums[layer], spread[...], repeat, width)
        sigma[layer] = jnp.broadcast_to(s, sigma.shape[1:])
        value[layer] = s * (u[layer] + by_layer(at[3], layer, own, other, acc, c, AHEAD))
        base = base + value[layer]
        c = base.astype(BF)
    half = keep.shape[1]
    mine, theirs = pick(at, *inputs)
    low = at[0] == 0
    for c, here, there in ((mine, keep, far_keep), (theirs, give, far_give)):
        c = c.astype(BF).astype(F32)
        here[...] = jnp.where(low, c[:, :half], c[:, half:]).astype(BF)
        there[...] = jnp.where(low, c[:, half:], c[:, :half]).astype(BF)
    g = g4[...]
    for layer in (1, 0):
        g = lower_of(width, at, layer, own, other, acc, g, sums[layer], sigma[layer][:, :1], value[layer])
    g_out[...] = g.astype(BF)


def send_kernel(width, at, own, other, g4, g_in, value, sums, sigma, keep, give, acc):
    g = jnp.where(at[4] == 1, g4[...], g_in[...].astype(F32))
    out = [None, None]
    for layer in (1, 0):
        s = sigma[layer][:, :1]
        out[layer] = g.astype(BF).astype(F32) * s
        if layer == 1:
            g = lower_of(width, at, 1, own, other, acc, g, sums[1], s, value[1])
    mine, theirs = pick(at, *out)
    keep[...] = mine.astype(BF)
    give[...] = theirs.astype(BF)


def chain_call(kernel, out, at, *args):
    rows, kv = args[2].shape[-2:]
    return call(
        kernel,
        out,
        in_specs=[pl.BlockSpec(memory_space=pltpu.SMEM)] + [pl.BlockSpec(memory_space=pltpu.VMEM)] * len(args),
        scratch_shapes=[pltpu.VMEM((rows, kv), F32)],
    )(at, *args)


def wgrad_first_kernel(at, turned, *refs):
    near, far, out, right = refs[:4], refs[4:8], refs[8], refs[9]
    for k in range(4):
        for z, r in enumerate((near[k], far[k])):
            begin = (k * 2 + z) * r.shape[0]
            right[begin : begin + r.shape[0], :] = r[...]
    wgrad_kernel((2,), at, turned, right, out)


def wgrad_kernel(ahead, at, turned, right, *outs):
    part = outs[0].shape[0]
    for j, out in zip(ahead, outs):
        rows = wide(lax.rem(at[2] + j, 4), part)
        out[...] = jnp.dot(turned[rows, :], right[...], preferred_element_type=F32).astype(BF)


AXES = ("zh", "co", "zl", "y", "x")


def move(v, where):
    flat = lambda d: (((d[0] * 2 + d[1]) * 2 + d[2]) * 4 + d[3] % 4) * 4 + d[4] % 4
    every = [(a, b, c, d, e) for a in range(2) for b in range(2) for c in range(2) for d in range(4) for e in range(4)]
    pairs = [(flat(d), flat(where(*d))) for d in every if where(*d) is not None]
    return lax.ppermute(v, AXES, pairs)


def ring(v, k, on_y):
    if k % 4 == 0:
        return v
    return move(v, lambda a, b, c, y, x: (a, b, c, y + k, x) if b == on_y else (a, b, c, y, x + k))


def to_g(v, k):
    return ring(v, k, 0)


def to_h(v, k):
    return ring(v, k, 1)


def ring_all(vs, way):
    return [vs[0] if k == 0 else to_g(vs[k], way * k) for k in range(4)]


def along_x(v, k):
    return v if k == 0 else move(v, lambda a, b, c, y, x: (a, b, c, y, x + k))


def to_z(v):
    return move(v, lambda a, b, c, y, x: (a, b, 1 - c, y, x))


def to_core(v):
    return move(v, lambda a, b, c, y, x: (a, 1 - b, c, y, x))


def to_z_core(v):
    return move(v, lambda a, b, c, y, x: (a, 1 - b, 1 - c, y, x))


def up(v):
    return move(v, lambda a, b, c, y, x: (1, b, c, y, x) if a == 0 else None)


def down(v):
    return move(v, lambda a, b, c, y, x: (0, b, c, y, x) if a == 1 else None)


def per_device(value_weight, norm_gain, mask_logits, gumbel_noise, stream_in, stream_grad):
    zh, co, zl, y, x = (lax.axis_index(n) for n in AXES)
    _, rows, width = stream_in.shape
    kv = value_weight.shape[2]
    head = kv // VHEADS
    repeat = width // kv
    part = value_weight.shape[1]
    own = zl * 16 + y * 4 + x
    first = co == 0
    at = jnp.stack([zl, jnp.where(first, y, x), jnp.where(first, x, y), co, zh])
    weight = value_weight[0]
    wide32 = shape((rows, kv), F32)
    half = shape((rows, kv), BF)

    stream = stream_in if INTERPRET else pltpu.with_memory_space_constraint(stream_in, HBM)
    far = far_half(at, stream)
    far = to_z(far)
    scaled, *quarters = masked_weights(jnp.stack([x, own]), mask_logits[0], gumbel_noise[0], weight, norm_gain)
    blocks = [to_h(scaled, k) for k in range(4)]
    quarters = [along_x(quarters[k], k) for k in range(4)]
    swapped = to_core(far)
    tokens = token_blocks(at, stream, far, swapped)
    tokens = [to_g(tokens[k], k) for k in range(4)]
    probs, ready = call(
        ready_kernel, (shape(mask_logits[0].shape, F32), shape(weight.shape, F32)), **small(4)
    )(jnp.stack([x, own]), mask_logits[0], gumbel_noise[0], weight, norm_gain)
    short = call(short_kernel, shape(quarters[0].shape, BF))(*quarters)
    short = jnp.stack([short, to_z(short)])
    short = jnp.stack([to_g(short, k) for k in range(4)])
    square = [to_h(short, k) for k in range(4)]
    swapped = [to_core(v) for v in square]
    n = call(functools.partial(square_kernel, 0), shape((kv, kv), BF), **small(4))(at, *square)
    n_other = call(functools.partial(square_kernel, 1), shape((kv, kv), BF), **small(4))(at, *swapped)

    u_far = partial_values(at, tokens, blocks, True)
    u_far = ring_all(u_far, -1)
    u_near = partial_values(at, tokens, blocks, False)
    u_near = ring_all(u_near, -1)
    far_keep, far_give = call(gathered_kernel, (half, half))(*u_far)
    far_mine = to_z(far_keep)
    far_theirs = to_z_core(far_give)
    mine, give = call(gathered_kernel, (wide32, half))(*u_near)
    theirs = to_core(give)
    y0, spread, g4 = token_sums(at[3:4], stream_in, stream_grad, head)

    two = shape((2, rows, kv), F32)
    u, c = chain_call(
        functools.partial(first_kernel, repeat, width),
        (two, half),
        at, n, n_other, mine, theirs, far_mine, far_theirs, y0, spread,
    )
    c_in = up(c)
    quarter = shape((rows, kv // 2), BF)
    value, sums, sigma, keep, give, far_keep, far_give, g = chain_call(
        functools.partial(turn_kernel, repeat, width),
        (two, two, shape((2, rows, head), F32)) + (quarter,) * 4 + (half,),
        at, n, n_other, u, y0, spread, c_in, g4,
    )
    g_in = down(g)
    cs = jnp.stack([
        jnp.concatenate([keep, to_core(give)]), jnp.concatenate([to_z(far_keep), to_z_core(far_give)])
    ])
    cs = [to_g(cs, k) for k in range(4)]
    keep, give = chain_call(
        functools.partial(send_kernel, width), (half, half),
        at, n, n_other, g4, g_in, value, sums, sigma,
    )
    near = to_core(give)
    far, far_give = to_z(keep), to_z_core(give)
    near = ring_all([jnp.concatenate([keep, near])] * 4, 1)
    far = ring_all([jnp.concatenate([far, far_give])] * 4, 1)
    turned = turn_over(at, tokens, cs)
    block = shape((part, kv), BF)
    t2, right = call(wgrad_first_kernel, [block, shape(turned.shape, BF)], **small(9))(at, turned, *near, *far)
    t2 = to_h(t2, 2)
    t1, t3 = call(functools.partial(wgrad_kernel, (1, 3)), [block] * 2, **small(2))(at, turned, right)
    t1, t3 = to_h(t1, 1), to_h(t3, 3)
    (t0,) = call(functools.partial(wgrad_kernel, (0,)), [block], **small(2))(at, turned, right)
    return logit_gradient(probs, ready, [t0, t1, t2, t3])[None]


def solution(mesh):
    fine = Mesh(mesh.devices.reshape(2, 2, 2, 4, 4), ("zh", "co", "zl", "y", "x"))
    dp = ("zl", "y", "x")

    return jax.shard_map(
        per_device,
        mesh=fine,
        in_specs=(
            P(LAYER, dp, None),
            P(LAYER, None),
            P(LAYER, None, dp, None),
            P(LAYER, None, dp, None),
            P(None, dp, None),
            P(None, dp, None),
        ),
        out_specs=P(LAYER, None, dp, None),
        check_vma=False,
    )
```

```python
import functools

import jax
import jax.numpy as jnp
from jax import lax
from jax.experimental import pallas as pl
from jax.experimental.pallas import tpu as pltpu
from jax.sharding import Mesh
from jax.sharding import PartitionSpec as P


VHEADS = 8
sharpness_divisor = 0.6666667
epsilon = 1e-05
BF = jnp.bfloat16
F32 = jnp.float32
INTERPRET = False
HBM = pltpu.HBM
KEEPS = ((0, 1), (0, 2), (0, 3), (1, 2), (1, 3), (2, 3))
LAYER = ("zh", "co")


def shape(dims, dtype):
    return jax.ShapeDtypeStruct(dims, dtype)


def call(kernel, out, **rest):
    params = pltpu.CompilerParams(vmem_limit_bytes=20 << 20)
    return pl.pallas_call(kernel, out_shape=out, interpret=INTERPRET, compiler_params=params, **rest)


def tiles(width, most=128):
    step = min(width, most)
    return [slice(i, i + step) for i in range(0, width, step)]


def by_tile(rows, width, most=128):
    cols = tiles(width, min(most, 128))
    return pltpu.VMEM((len(cols), rows, cols[0].stop), F32)


def pattern_probs(logits, noise, s):
    expo = [
        jnp.exp((logits[k, :, s].astype(F32) + noise[k, :, s].astype(F32)) * (1.0 / sharpness_divisor))
        for k in range(6)
    ]
    inverse = 1.0 / (((expo[0] + expo[1]) + (expo[2] + expo[3])) + (expo[4] + expo[5]))
    return [e * inverse for e in expo]


def gain_column(index, gain, rows):
    row = gain[:, pl.ds(pl.multiple_of(index * rows, rows), rows)].astype(F32)
    return jnp.broadcast_to(row, (8, rows)).T[:, :1]


def mask_kernel(at, logits, noise, weight, gain, scaled, q0, q1, q2, q3, rows):
    column = gain_column(at[1], gain, weight.shape[0])
    for i, s in enumerate(tiles(weight.shape[1])):
        p = pattern_probs(logits, noise, s)
        for r in range(4):
            kept = [p[k] for k in range(6) if r in KEEPS[k]]
            rows.at[i][pl.ds(r, kept[0].shape[0], stride=4), :] = kept[0] + kept[1] + kept[2]
        value = weight[:, s].astype(F32) * rows[i] * column
        scaled[:, s] = value.astype(BF)
        rows[i] = value
        quarter = q0.shape[0]
        for k, q in enumerate((q0, q1, q2, q3)):
            begin = pl.multiple_of(lax.rem(at[0] + k, 4) * quarter, quarter)
            one = rows.at[i][pl.ds(begin, quarter), :]
            two = rows.at[i][pl.ds(begin + 4 * quarter, quarter), :]
            q[:, s] = (one + two).astype(BF)


def masked_weights(at, logits, noise, weight, gain):
    n, kv = weight.shape
    return call(
        mask_kernel,
        (shape((n, kv), BF),) + (shape((n // 8, kv), BF),) * 4,
        in_specs=[pl.BlockSpec(memory_space=pltpu.SMEM)] + [pl.BlockSpec(memory_space=pltpu.VMEM)] * 4,
        scratch_shapes=[by_tile(n, kv)],
    )(at, logits, noise, weight, gain)


def ready_kernel(at, logits, noise, weight, gain, probs, ready):
    column = gain_column(at[1], gain, weight.shape[0]) * (1.0 / sharpness_divisor)
    for s in tiles(weight.shape[1]):
        for k, p in enumerate(pattern_probs(logits, noise, s)):
            probs[k, :, s] = p
        ready[:, s] = weight[:, s].astype(F32) * column


def final_kernel(probs, ready, *refs):
    parts, out, rows, done, sems = refs[:-4], *refs[-4:]
    copies = []
    for i, s in enumerate(tiles(ready.shape[1])):
        total = (parts[0][:, s].astype(F32) + parts[1][:, s].astype(F32)) + (
            parts[2][:, s].astype(F32) + parts[3][:, s].astype(F32)
        )
        rows[i] = total * ready[:, s]
        d = [rows.at[i][pl.ds(r, probs.shape[1], stride=4), :] for r in range(4)]
        p = [probs[k, :, s] for k in range(6)]
        dprob = [d[a] + d[b] for a, b in KEEPS]
        mean = p[0] * dprob[0]
        for k in range(1, 6):
            mean = mean + p[k] * dprob[k]
        for k in range(6):
            done[i, k] = (p[k] * (dprob[k] - mean)).astype(BF)
        copies.append(pltpu.make_async_copy(done.at[i], out.at[:, :, s], sems.at[i]))
        copies[-1].start()
    for copy in copies:
        copy.wait()


def logit_gradient(probs, ready, parts):
    count = len(tiles(ready.shape[1]))
    tile = ready.shape[1] // count
    return call(
        final_kernel,
        shape(probs.shape, BF),
        out_specs=pl.BlockSpec(memory_space=pl.ANY),
        scratch_shapes=[
            by_tile(*ready.shape),
            pltpu.VMEM((count, *probs.shape[:2], tile), BF),
            pltpu.SemaphoreType.DMA((count,)),
        ],
    )(probs, ready, *parts)


def run_copies(copies, sems):
    copies = [pltpu.make_async_copy(src, dst, sems.at[i]) for i, (src, dst) in enumerate(copies)]
    for copy in copies:
        copy.start()
    for copy in copies:
        copy.wait()


def wide(index, part):
    return pl.ds(pl.multiple_of(index * part, part), part)


def place(core, zl, g, h):
    return zl * 16 + jnp.where(core == 0, g * 4 + h, h * 4 + g)


def slice_kernel(at, tokens, out, sem):
    width = out.shape[1]
    source = wide(1 - at[0], width)
    copy = pltpu.make_async_copy(tokens.at[at[3], :, source], out, sem)
    copy.start()
    copy.wait()


def far_half(at, tokens):
    rows, width = tokens.shape[1:]
    return call(
        slice_kernel,
        shape((rows, width // 2), BF),
        in_specs=[pl.BlockSpec(memory_space=pltpu.SMEM), pl.BlockSpec(memory_space=HBM)],
        out_specs=pl.BlockSpec(memory_space=pltpu.VMEM),
        scratch_shapes=[pltpu.SemaphoreType.DMA],
    )(at, tokens)


def blocks_kernel(at, tokens, mine, other, o0, o1, o2, o3, sems):
    zl, g, core = at[0], at[1], at[3]
    rows, width = tokens.shape[1:]
    part = width // 32
    copies = []
    for k, out in enumerate((o0, o1, o2, o3)):
        for i in range(4):
            near = wide(place(core, zl, lax.rem(g + k, 4), i), part)
            far = wide(place(core, 0, lax.rem(g + k, 4), i), part)
            sources = (tokens.at[core, :, near], tokens.at[1 - core, :, near], mine.at[:, far], other.at[:, far])
            for r, source in enumerate(sources):
                copies.append((source, out.at[pl.ds(r * rows, rows), pl.ds(i * part, part)]))
    run_copies(copies, sems)


def token_blocks(at, tokens, mine, other):
    rows, width = tokens.shape[1:]
    block = pl.BlockSpec(memory_space=pl.ANY)
    return call(
        blocks_kernel,
        (shape((4 * rows, width // 8), BF),) * 4,
        in_specs=[pl.BlockSpec(memory_space=pltpu.SMEM), pl.BlockSpec(memory_space=HBM), block, block],
        out_specs=(pl.BlockSpec(memory_space=pltpu.VMEM),) * 4,
        scratch_shapes=[pltpu.SemaphoreType.DMA((64,))],
    )(at, tokens, mine, other)


def sums_kernel(repeat, head, core, tokens, grads, y0, spread, g4):
    t = tokens[0]
    pieces = [t[:, r * head : (r + 1) * head].astype(F32) for r in range(repeat)]
    total = functools.reduce(lambda a, b: a + b, pieces)
    mean = total * (1.0 / repeat)
    squares = functools.reduce(lambda a, b: a + b, [(p - mean) * (p - mean) for p in pieces])
    y0[...] = total

    @pl.when(pl.program_id(0) == 0)
    def _():
        spread[...] = squares

    @pl.when(pl.program_id(0) != 0)
    def _():
        spread[...] += squares

    g = grads[0]
    g4[...] = functools.reduce(
        lambda a, b: a + b, [g[:, r * head : (r + 1) * head].astype(F32) for r in range(repeat)]
    )


def token_sums(core, tokens, grads, head):
    rows, width = tokens.shape[1:]
    span = width // VHEADS
    block = pl.BlockSpec((1, rows, span), lambda h, core: (core[0], 0, h))
    narrow = pl.BlockSpec((rows, head), lambda h, core: (0, h))
    return call(
        functools.partial(sums_kernel, span // head, head),
        (
            shape((rows, VHEADS * head), F32),
            shape((rows, head), F32),
            shape((rows, VHEADS * head), F32),
        ),
        grid_spec=pltpu.PrefetchScalarGridSpec(
            num_scalar_prefetch=1,
            grid=(VHEADS,),
            in_specs=[block, block],
            out_specs=(
                narrow,
                pl.BlockSpec((rows, head), lambda h, core: (0, 0)),
                narrow,
            ),
        ),
    )(core, tokens, grads)


def small(count):
    vmem = pl.BlockSpec(memory_space=pltpu.VMEM)
    return dict(in_specs=[pl.BlockSpec(memory_space=pltpu.SMEM)] + [vmem] * count)


def values_kernel(far, at, *refs):
    tokens, w, outs = refs[:4], refs[4:8], refs[8:]
    part = w[0].shape[0]
    rows = outs[0].shape[0]
    mine = slice(rows, 2 * rows) if far else slice(0, rows)
    for k in range(0, 4, 2):
        total = None
        for j in range(4):
            cols = wide(lax.rem(at[2] - j + 4, 4), part)
            lhs = jnp.concatenate([tokens[k][mine, cols], tokens[k + 1][mine, cols]], 0)
            term = jnp.dot(lhs, w[j][...], preferred_element_type=F32)
            total = term if total is None else total + term
        outs[k][...] = total[:rows].astype(BF)
        outs[k + 1][...] = total[rows:].astype(BF)


def partial_values(at, tokens, blocks, far):
    out = [shape((tokens[0].shape[0] // 2, blocks[0].shape[1]), BF)] * 4
    return call(functools.partial(values_kernel, far), out, **small(8))(at, *tokens, *blocks)


def gathered_kernel(m0, m1, m2, m3, keep, give):
    rows = keep.shape[0]
    for i, out in enumerate((keep, give)):
        p = [m[i * rows : (i + 1) * rows, :].astype(F32) for m in (m0, m1, m2, m3)]
        out[...] = ((p[0] + p[1]) + (p[2] + p[3])).astype(out.dtype)


def turn_over_kernel(at, *refs):
    tokens, cs, out = refs[:4], refs[4:8], refs[8]
    rows = tokens[0].shape[0] // 2
    head = cs[0].shape[2] // 4
    for k in range(4):
        for z in range(2):
            add = []
            for i in range(4):
                which = jnp.where(at[3] == 0, at[1], i)
                c = cs[k][z, :, wide(which, head)].astype(F32)
                add += [c, c]
            x = tokens[k][z * rows : (z + 1) * rows, :].astype(F32) + jnp.concatenate(add, 1)
            begin = (k * 2 + z) * rows
            out[:, begin : begin + rows] = x.astype(BF).T


def turn_over(at, tokens, cs):
    rows, span = tokens[0].shape
    return call(turn_over_kernel, shape((span, 4 * rows), BF), **small(8))(at, *tokens, *cs)


def short_kernel(q0, q1, q2, q3, out):
    total = (q0[...].astype(F32) + q1[...].astype(F32)) + (q2[...].astype(F32) + q3[...].astype(F32))
    out[...] = total.astype(BF)


def square_kernel(swapped, at, n0, n1, n2, n3, out):
    quarter = n0.shape[2]
    zl, g, h, core = (at[i] for i in range(4))
    if swapped:
        g, h, core = h, g, 1 - core
    for j, n in enumerate((n0, n1, n2, n3)):
        for k in range(4):
            for z in range(2):
                there = zl if z == 0 else 1 - zl
                at_row = place(core, there, lax.rem(g - k + 4, 4), lax.rem(h - j + 4, 4))
                out[wide(at_row, quarter), :] = n[k, z]


def scale_of(sums, spread, repeat, width):
    mean = jnp.sum(spread, -1, keepdims=True) + jnp.sum(sums * sums, -1, keepdims=True) * (1.0 / repeat)
    return lax.rsqrt(mean * (1.0 / width) + epsilon)


def by_layer(core, layer, own, other, acc, v, dims):
    @pl.when(core == layer)
    def _():
        acc[...] = lax.dot_general(v, own[...], (dims, ((), ())), preferred_element_type=F32)

    @pl.when(core != layer)
    def _():
        acc[...] = lax.dot_general(v, other[...], (dims, ((), ())), preferred_element_type=F32)

    return acc[...]


AHEAD = ((1,), (0,))
BEHIND = ((1,), (1,))


def first_kernel(repeat, width, at, own, other, mine, theirs, far_mine, far_theirs, y0, spread, u, c_out, acc):
    one = mine[...] + far_mine[...].astype(F32)
    two = theirs[...].astype(F32) + far_theirs[...].astype(F32)
    u[0] = jnp.where(at[3] == 0, one, two)
    u[1] = jnp.where(at[3] == 0, two, one)
    c = scale_of(y0[...], spread[...], repeat, width) * u[0]
    sums = y0[...] + repeat * c
    value = u[1] + by_layer(at[3], 1, own, other, acc, c.astype(BF), AHEAD)
    c_out[...] = (c + scale_of(sums, spread[...], repeat, width) * value).astype(BF)


def pre_kernel(at, own, other, g4, du, acc):
    du[...] = by_layer(at[3], 1, own, other, acc, g4[...].astype(BF), BEHIND)


def lower_of(width, at, layer, own, other, acc, g, sums, sigma, value, du=None):
    vg = g.astype(BF)
    if du is None:
        du = by_layer(at[3], layer, own, other, acc, vg, BEHIND)
    dot = jnp.sum(vg.astype(F32) * value, -1, keepdims=True) * (1.0 / width)
    return g + sigma * du - sigma * sigma * dot * sums


def pick(at, a, b):
    first = at[3] == 0
    return jnp.where(first, a, b), jnp.where(first, b, a)


def turn_kernel(
    repeat, width, at, own, other, u, y0, spread, c_in, g4, du,
    value, sums, sigma, keep, give, far_keep, far_give, g_out, acc,
):
    c = c_in[...]
    base = c.astype(F32)
    inputs = []
    for layer in range(2):
        inputs.append(base)
        sums[layer] = y0[...] + repeat * base
        s = scale_of(sums[layer], spread[...], repeat, width)
        sigma[layer] = jnp.broadcast_to(s, sigma.shape[1:])
        value[layer] = s * (u[layer] + by_layer(at[3], layer, own, other, acc, c, AHEAD))
        base = base + value[layer]
        c = base.astype(BF)
    half = keep.shape[1]
    mine, theirs = pick(at, *inputs)
    low = at[0] == 0
    for c, here, there in ((mine, keep, far_keep), (theirs, give, far_give)):
        c = c.astype(BF).astype(F32)
        here[...] = jnp.where(low, c[:, :half], c[:, half:]).astype(BF)
        there[...] = jnp.where(low, c[:, half:], c[:, :half]).astype(BF)
    g = g4[...]
    for layer in (1, 0):
        g = lower_of(width, at, layer, own, other, acc, g, sums[layer], sigma[layer][:, :1], value[layer], du[...] if layer else None)
    g_out[...] = g.astype(BF)


def send_kernel(width, at, own, other, g4, g_in, value, sums, sigma, keep, give, acc):
    g = jnp.where(at[4] == 1, g4[...], g_in[...].astype(F32))
    out = [None, None]
    for layer in (1, 0):
        s = sigma[layer][:, :1]
        out[layer] = g.astype(BF).astype(F32) * s
        if layer == 1:
            g = lower_of(width, at, 1, own, other, acc, g, sums[1], s, value[1])
    mine, theirs = pick(at, *out)
    keep[...] = mine.astype(BF)
    give[...] = theirs.astype(BF)


def chain_call(kernel, out, at, *args):
    rows, kv = args[2].shape[-2:]
    return call(
        kernel,
        out,
        in_specs=[pl.BlockSpec(memory_space=pltpu.SMEM)] + [pl.BlockSpec(memory_space=pltpu.VMEM)] * len(args),
        scratch_shapes=[pltpu.VMEM((rows, kv), F32)],
    )(at, *args)


def wgrad_first_kernel(at, turned, *refs):
    near, far, out, right = refs[:4], refs[4:8], refs[8], refs[9]
    for k in range(4):
        for z, r in enumerate((near[k], far[k])):
            begin = (k * 2 + z) * r.shape[0]
            right[begin : begin + r.shape[0], :] = r[...]
    wgrad_kernel((2,), at, turned, right, out)


def wgrad_kernel(ahead, at, turned, right, *outs):
    part = outs[0].shape[0]
    for j, out in zip(ahead, outs):
        rows = wide(lax.rem(at[2] + j, 4), part)
        out[...] = jnp.dot(turned[rows, :], right[...], preferred_element_type=F32).astype(BF)


AXES = ("zh", "co", "zl", "y", "x")


def move(v, where):
    flat = lambda d: (((d[0] * 2 + d[1]) * 2 + d[2]) * 4 + d[3] % 4) * 4 + d[4] % 4
    every = [(a, b, c, d, e) for a in range(2) for b in range(2) for c in range(2) for d in range(4) for e in range(4)]
    pairs = [(flat(d), flat(where(*d))) for d in every if where(*d) is not None]
    return lax.ppermute(v, AXES, pairs)


def ring(v, k, on_y):
    if k % 4 == 0:
        return v
    return move(v, lambda a, b, c, y, x: (a, b, c, y + k, x) if b == on_y else (a, b, c, y, x + k))


def to_g(v, k):
    return ring(v, k, 0)


def to_h(v, k):
    return ring(v, k, 1)


def ring_all(vs, way):
    return [vs[0] if k == 0 else to_g(vs[k], way * k) for k in range(4)]


def along_x(v, k):
    return v if k == 0 else move(v, lambda a, b, c, y, x: (a, b, c, y, x + k))


def to_z(v):
    return move(v, lambda a, b, c, y, x: (a, b, 1 - c, y, x))


def to_core(v):
    return move(v, lambda a, b, c, y, x: (a, 1 - b, c, y, x))


def to_z_core(v):
    return move(v, lambda a, b, c, y, x: (a, 1 - b, 1 - c, y, x))


def up(v):
    return move(v, lambda a, b, c, y, x: (1, b, c, y, x) if a == 0 else None)


def down(v):
    return move(v, lambda a, b, c, y, x: (0, b, c, y, x) if a == 1 else None)


def per_device(value_weight, norm_gain, mask_logits, gumbel_noise, stream_in, stream_grad):
    zh, co, zl, y, x = (lax.axis_index(n) for n in AXES)
    _, rows, width = stream_in.shape
    kv = value_weight.shape[2]
    head = kv // VHEADS
    repeat = width // kv
    part = value_weight.shape[1]
    own = zl * 16 + y * 4 + x
    first = co == 0
    at = jnp.stack([zl, jnp.where(first, y, x), jnp.where(first, x, y), co, zh])
    weight = value_weight[0]
    wide32 = shape((rows, kv), F32)
    half = shape((rows, kv), BF)

    stream = stream_in if INTERPRET else pltpu.with_memory_space_constraint(stream_in, HBM)
    far = far_half(at, stream)
    far = to_z(far)
    scaled, *quarters = masked_weights(jnp.stack([x, own]), mask_logits[0], gumbel_noise[0], weight, norm_gain)
    blocks = [to_h(scaled, k) for k in range(4)]
    quarters = [along_x(quarters[k], k) for k in range(4)]
    swapped = to_core(far)
    tokens = token_blocks(at, stream, far, swapped)
    tokens = [to_g(tokens[k], k) for k in range(4)]
    probs, ready = call(
        ready_kernel, (shape(mask_logits[0].shape, F32), shape(weight.shape, F32)), **small(4)
    )(jnp.stack([x, own]), mask_logits[0], gumbel_noise[0], weight, norm_gain)
    short = call(short_kernel, shape(quarters[0].shape, BF))(*quarters)
    short = jnp.stack([short, to_z(short)])
    short = jnp.stack([to_g(short, k) for k in range(4)])
    square = [to_h(short, k) for k in range(4)]
    swapped = [to_core(v) for v in square]
    n = call(functools.partial(square_kernel, 0), shape((kv, kv), BF), **small(4))(at, *square)
    n_other = call(functools.partial(square_kernel, 1), shape((kv, kv), BF), **small(4))(at, *swapped)

    u_far = partial_values(at, tokens, blocks, True)
    u_far = ring_all(u_far, -1)
    u_near = partial_values(at, tokens, blocks, False)
    u_near = ring_all(u_near, -1)
    far_keep, far_give = call(gathered_kernel, (half, half))(*u_far)
    far_mine = to_z(far_keep)
    far_theirs = to_z_core(far_give)
    mine, give = call(gathered_kernel, (wide32, half))(*u_near)
    theirs = to_core(give)
    y0, spread, g4 = token_sums(at[3:4], stream_in, stream_grad, head)

    two = shape((2, rows, kv), F32)
    u, c = chain_call(
        functools.partial(first_kernel, repeat, width),
        (two, half),
        at, n, n_other, mine, theirs, far_mine, far_theirs, y0, spread,
    )
    c_in = up(c)
    du = chain_call(pre_kernel, wide32, at, n, n_other, g4)
    quarter = shape((rows, kv // 2), BF)
    value, sums, sigma, keep, give, far_keep, far_give, g = chain_call(
        functools.partial(turn_kernel, repeat, width),
        (two, two, shape((2, rows, head), F32)) + (quarter,) * 4 + (half,),
        at, n, n_other, u, y0, spread, c_in, g4, du,
    )
    g_in = down(g)
    cs = jnp.stack([
        jnp.concatenate([keep, to_core(give)]), jnp.concatenate([to_z(far_keep), to_z_core(far_give)])
    ])
    cs = [to_g(cs, k) for k in range(4)]
    keep, give = chain_call(
        functools.partial(send_kernel, width), (half, half),
        at, n, n_other, g4, g_in, value, sums, sigma,
    )
    near = to_core(give)
    far, far_give = to_z(keep), to_z_core(give)
    near = ring_all([jnp.concatenate([keep, near])] * 4, 1)
    far = ring_all([jnp.concatenate([far, far_give])] * 4, 1)
    turned = turn_over(at, tokens, cs)
    block = shape((part, kv), BF)
    t2, right = call(wgrad_first_kernel, [block, shape(turned.shape, BF)], **small(9))(at, turned, *near, *far)
    t2 = to_h(t2, 2)
    t1, t3 = call(functools.partial(wgrad_kernel, (1, 3)), [block] * 2, **small(2))(at, turned, right)
    t1, t3 = to_h(t1, 1), to_h(t3, 3)
    (t0,) = call(functools.partial(wgrad_kernel, (0,)), [block], **small(2))(at, turned, right)
    return logit_gradient(probs, ready, [t0, t1, t2, t3])[None]


def solution(mesh):
    fine = Mesh(mesh.devices.reshape(2, 2, 2, 4, 4), ("zh", "co", "zl", "y", "x"))
    dp = ("zl", "y", "x")

    return jax.shard_map(
        per_device,
        mesh=fine,
        in_specs=(
            P(LAYER, dp, None),
            P(LAYER, None),
            P(LAYER, None, dp, None),
            P(LAYER, None, dp, None),
            P(None, dp, None),
            P(None, dp, None),
        ),
        out_specs=P(LAYER, None, dp, None),
        check_vma=False,
    )
```
